32 devices in a mesh: rep: 2 (over y), ep: 8 (over z, x), tp: 2 (over core).
Axes of the slice: x: 2, y: 2, z: 4, core: 2. Of those that a mesh axis runs over, the one named last changes fastest.
Arguments:
- tokens: bfloat16 [2048, 3584], P(('rep', 'ep'), 'tp'), parts along dimension 0, may hold values from -6 to 6
- expert_ids: int32 [2048, 8], P(('rep', 'ep')), parts along dimension 0, may hold values from 0 to 63, all different within a row; in each aligned block of 512 rows (0 to 511, 512 to 1023, ...) at most 128 rows name the same one
- gate_values: float32 [2048, 8], P(('rep', 'ep')), parts along dimension 0, may hold values from 0.1 to 1
- group_counts: int32 [4], P('rep'), parts along dimension 0, may hold values from 256 to 512
- gate_weight: bfloat16 [14336, 2560], P(('rep', 'ep'), 'tp'), parts along dimension 0, may hold values from -0.09375 to 0.09375
- up_weight: bfloat16 [14336, 2560], P(('rep', 'ep'), 'tp'), parts along dimension 0, may hold values from -0.09375 to 0.09375
- down_weight: bfloat16 [14336, 2560], P(('rep', 'ep'), 'tp'), parts along dimension 0, may hold values from -0.125 to 0.125
Outputs:
- expert_output: bfloat16 [2048, 3584], P(('rep', 'ep'), 'tp'), parts along dimension 0
The draws below stay inside these ranges and needn't reach their ends.
There are 2 independent parts, one for each index of `rep`. The reference program is written for one: setup_inputs(seed, part) draws one part's arguments, and reference() takes and returns one part's arrays. A program takes and returns all parts, laid end to end along the dimension named above; each array names one. Nothing has to cross between parts.
Inputs may be any that keep to these rules, and one draw needn't show every extreme that they name: `expert_ids`: each row names 8 different experts; within the 512 rows of one rollout group no expert is named by more than 128 rows.
All inputs are finite; a program needn't handle non-finite values.
Results may differ from the reference program's by a relative error of at most 0.014.
Values may be sent and summed in bfloat16 or wider, within the bound.
A program may use at most 128 MiB of HBM per device.

```python
import math
import jax
import jax.numpy as jnp
import numpy as np
from jax import lax

D = 3584
FF = 2560
EXPERTS = 64
TOPK = 8
WAVE = 2
MEMBERS = 8
TOK_G = 512
CAP = 128
GROUPS = 2
TOKENS = 1024


def block_scale(rng, dims, split, least, top_value):
    loudness = 1.0
    for axis_at, parts in split:
        heights = jax.random.uniform(jax.random.fold_in(jax.random.fold_in(rng, 6), axis_at), (parts,), jnp.float32, least / len(split), top_value / len(split))
        loudness = loudness * jnp.repeat(jnp.exp(heights), dims[axis_at] // parts).reshape((-1,) + (1,) * (len(dims) - 1 - axis_at))
    return loudness


def routed_block(own_key, own, number, rows, count, top, most, slope):
    sequence = jax.random.permutation(own_key, count)
    crowded, common = shares(count, rows * top, most, slope, True), shares(count, rows * top, most, slope, False)
    places = jnp.arange(count)

    def named(tallies, rotation):
        used = int((tallies > 0).sum())
        fixed = max(1, used // 4)
        moved = fixed + (places - fixed + rotation * (used - fixed)) % max(1, count - fixed)
        return jnp.zeros((count,), jnp.int32).at[sequence[jnp.where(places < fixed, places, moved)]].set(jnp.asarray(tallies, jnp.int32))

    tallies = jnp.where(number % 4 == 0, named(crowded, number // 4), named(common, number - number // 4 - 1))
    mixed = jax.random.permutation(jax.random.fold_in(own, 3), count)
    source_of, taker = mixed[0:count // 2 * 2:2], mixed[1:count // 2 * 2:2]
    room = jnp.minimum(tallies[source_of] - 1, most - tallies[taker]) // 2
    room = jnp.where((source_of == sequence[0]) | (taker == sequence[0]) | (tallies[taker] == 0), 0, jnp.maximum(room, 0))
    moved = jax.random.randint(jax.random.fold_in(own, 4), (count // 2,), 0, 1 << 20) % (room + 1)
    tallies = tallies.at[source_of].add(-moved).at[taker].add(moved)
    members = jnp.searchsorted(jnp.cumsum(tallies), jnp.arange(rows * top), side="right").astype(jnp.int32)
    grid = members.reshape(top, rows).T
    grid = grid[jax.random.permutation(jax.random.fold_in(own, 1), rows)]
    rotation = jax.random.randint(jax.random.fold_in(own, 2), (rows, 1), 0, top)
    return jnp.take_along_axis(grid, (jnp.arange(top)[None, :] + rotation) % top, axis=1)


def shares(count, total, bound, lean, full):
    weights = [(1 << 20) // math.isqrt(grade ** lean) + 1 for grade in range(1, count + 1)]
    largest = bound if full else min(bound, max(-(-total // count), total * weights[0] // sum(weights)))
    least = 1 if total - largest >= count - 1 else 0
    holding, rest = [largest] + [least] * (count - 1), total - largest - least * (count - 1)
    while rest > 0:
        free = [i for i in range(1, count) if holding[i] < largest] or [i for i in range(1, count) if holding[i] < bound]
        pool, left = sum([weights[i] for i in free]), rest
        for i in free:
            extra = min(bound - holding[i], max(1, left * weights[i] // pool), rest)
            holding[i] = holding[i] + extra
            rest = rest - extra
    return np.array(holding)


def scatter_about(stream_key, dims, width, bound, shards=(), kind=jnp.bfloat16):
    values = width * jax.random.normal(stream_key, dims, jnp.float32)
    if shards:
        values = values * block_scale(stream_key, dims, shards, -0.22, 0.18)
    return jnp.clip(values, -bound, bound).astype(kind)


def setup_inputs(seed: int = 0, part: int = 0) -> dict:
    splits = jax.random.split(jax.random.key(seed), 8)
    own_keys = jax.random.split(jax.random.fold_in(splits[7], part), 8)
    tokens = scatter_about(own_keys[0], (TOKENS, D), 1.0, 6.0, ((0, 8), (1, 2)))
    expert_ids_keys = jax.random.split(jax.random.fold_in(own_keys[1], 1), TOKENS // TOK_G)
    expert_ids_turns = jax.random.permutation(jax.random.fold_in(own_keys[1], 3), TOKENS // TOK_G)
    expert_ids = jax.vmap(lambda own, number: routed_block(jax.random.fold_in(own_keys[1], 2), own, number, TOK_G, EXPERTS, TOPK, CAP, 2))(expert_ids_keys, expert_ids_turns).reshape((TOKENS, TOPK))
    gate_values = jnp.clip(0.1 + 0.9 * jax.random.uniform(own_keys[2], (TOKENS, TOPK), jnp.float32) ** block_scale(own_keys[2], (TOKENS, TOPK), ((0, 8),), -0.2, 0.2), 0.1, 1.0)
    group_counts = jax.random.randint(own_keys[3], (GROUPS,), TOK_G // 2, TOK_G + 1).astype(jnp.int32)
    gate_weight = scatter_about(own_keys[4], (WAVE * D, FF), D ** -0.5, 0.09375, ((0, 8), (1, 2)))
    up_weight = scatter_about(own_keys[5], (WAVE * D, FF), D ** -0.5, 0.09375, ((0, 8), (1, 2)))
    down_weight = scatter_about(own_keys[6], (WAVE * D, FF), FF ** -0.5, 0.125, ((0, 8), (1, 2)))
    return dict(tokens=tokens, expert_ids=expert_ids, gate_values=gate_values, group_counts=group_counts, gate_weight=gate_weight, up_weight=up_weight, down_weight=down_weight)


def dispatch_slots(expert_ids, gate_values, live_count, expert):
    row_index = jnp.arange(TOK_G, dtype=jnp.int32)
    live_rows = row_index < live_count
    hit_mask = expert_ids == expert
    selected = jnp.logical_and(jnp.any(hit_mask, axis=1), live_rows)
    row_weight = jnp.sum(jnp.where(hit_mask, gate_values, jnp.float32(0.0)), axis=1)
    position = jnp.cumsum(selected.astype(jnp.int32)) - 1
    slot_index = jnp.arange(CAP, dtype=jnp.int32)
    slot_match = jnp.logical_and(position[None, :] == slot_index[:, None], selected[None, :])
    slot_rows = jnp.sum(jnp.where(slot_match, row_index[None, :], 0), axis=1).astype(jnp.int32)
    slot_valid = jnp.any(slot_match, axis=1)
    slot_weight = jnp.where(slot_valid, row_weight[slot_rows], jnp.float32(0.0))
    return slot_rows, slot_weight


def one_group(group_tokens, expert_ids, gate_values, live_count, gate_weight, up_weight, down_weight):
    slice_width = FF // MEMBERS
    partials = jnp.zeros((MEMBERS, TOK_G, D), jnp.float32)
    for expert in range(WAVE):
        slot_rows, slot_weight = dispatch_slots(expert_ids, gate_values, live_count, expert)
        expert_rows = group_tokens[slot_rows]
        gate_act = jnp.dot(expert_rows, gate_weight[expert], preferred_element_type=jnp.float32)
        up_act = jnp.dot(expert_rows, up_weight[expert], preferred_element_type=jnp.float32)
        hidden = (jax.nn.silu(gate_act) * up_act).astype(jnp.bfloat16)
        for member in range(MEMBERS):
            hidden_piece = hidden[:, member * slice_width:(member + 1) * slice_width]
            down_piece = down_weight[expert][:, member * slice_width:(member + 1) * slice_width]
            projected = lax.dot_general(hidden_piece, down_piece, (((1,), (1,)), ((), ())), preferred_element_type=jnp.float32)
            partials = partials.at[member, slot_rows].add(slot_weight[:, None] * projected)
    rounded = lax.optimization_barrier(partials.astype(jnp.bfloat16)).astype(jnp.float32)
    return jnp.sum(rounded, axis=0).astype(jnp.bfloat16)


def reference(tokens, expert_ids, gate_values, group_counts, gate_weight, up_weight, down_weight):
    gate_blocks = gate_weight.reshape(WAVE, D, FF)
    up_blocks = up_weight.reshape(WAVE, D, FF)
    down_blocks = down_weight.reshape(WAVE, D, FF)

    def per_group(packed):
        group_tokens, group_ids, group_gates, live_count = packed
        return one_group(group_tokens, group_ids, group_gates, live_count, gate_blocks, up_blocks, down_blocks)

    combined = lax.map(per_group, (tokens.reshape(GROUPS, TOK_G, D), expert_ids.reshape(GROUPS, TOK_G, TOPK), gate_values.reshape(GROUPS, TOK_G, TOPK), group_counts))
    return combined.reshape(TOKENS, D)
```

```python
import functools

import jax
import jax.numpy as jnp
from jax import lax
from jax.experimental import pallas as pl
from jax.experimental.pallas import tpu as pltpu
from jax.sharding import PartitionSpec as P

D = 3584
FF = 2560
WAVE = 2
MEMBERS = 8
GROUP_EP = 4
MESH = pl.DeviceIdType.MESH
TOK_G = 512
CAP = 128


def as_sent(array):

    def short(part):
        return part.astype(jnp.bfloat16) if part.dtype == jnp.float32 else part

    return jax.tree.map(short, array)


def swapped(array, axis, distance):
    return lax.ppermute(array, axis, [(i, i ^ 1 << distance) for i in range(lax.axis_size(axis))])


def dispatch_slots(expert_ids, gate_values, live_count, expert):
    row_index = jnp.arange(TOK_G, dtype=jnp.int32)
    live_rows = row_index < live_count
    hit_mask = expert_ids == expert
    selected = jnp.logical_and(jnp.any(hit_mask, axis=1), live_rows)
    row_weight = jnp.sum(jnp.where(hit_mask, gate_values, jnp.float32(0.0)), axis=1)
    position = jnp.cumsum(selected.astype(jnp.int32)) - 1
    slot_index = jnp.arange(CAP, dtype=jnp.int32)
    slot_match = jnp.logical_and(position[None, :] == slot_index[:, None], selected[None, :])
    slot_rows = jnp.sum(jnp.where(slot_match, row_index[None, :], 0), axis=1)
    slot_valid = jnp.any(slot_match, axis=1)
    slot_weight = jnp.where(slot_valid, row_weight[slot_rows], jnp.float32(0.0))
    return (slot_rows, slot_weight)


def shards(tokens, expert_ids, gate_values, group_counts, gate_weight, up_weight, down_weight):
    ep_index = lax.axis_index("ep")
    slice_width = FF // MEMBERS
    group_bits = GROUP_EP.bit_length() - 1
    weight_stack = jnp.stack([gate_weight, up_weight, down_weight])
    rows_held = weight_stack.shape[1]
    pieces = weight_stack.shape[2] // slice_width
    slice_blocks = weight_stack.reshape(3, rows_held, pieces, slice_width).transpose(0, 2, 1, 3)
    fan_out = lax.axis_size("ep") // pieces
    outgoing = jnp.tile(slice_blocks, (1, fan_out, 1, 1))
    arrived = lax.all_to_all(outgoing, "ep", split_axis=1, concat_axis=1, tiled=True)
    columns = arrived.reshape(3, -1, slice_width)
    features = lax.all_gather(tokens, "tp", axis=1, tiled=True)
    group_data = (features, expert_ids, gate_values)
    for bit_level in range(group_bits):
        received = jax.tree.map(
            lambda part, own: part.astype(own.dtype),
            swapped(as_sent(group_data), "ep", bit_level),
            group_data,
        )
        upper_half = ep_index >> bit_level & 1 == 1
        group_data = tuple(
            (
                jnp.where(
                    upper_half, jnp.concatenate([other, own], 0), jnp.concatenate([own, other], 0)
                )
                for own, other in zip(group_data, received)
            )
        )
    group_tokens, group_ids, group_gates = group_data
    live_count = lax.dynamic_index_in_dim(group_counts, ep_index // GROUP_EP, keepdims=False)
    partials = jnp.zeros((group_tokens.shape[0], D), jnp.float32)
    for expert in range(WAVE):
        slot_rows, slot_weight = dispatch_slots(group_ids, group_gates, live_count, expert)
        expert_rows = group_tokens[slot_rows]
        gate_cols = columns[0, expert * D : (expert + 1) * D]
        up_cols = columns[1, expert * D : (expert + 1) * D]
        down_cols = columns[2, expert * D : (expert + 1) * D]
        gate_act = jnp.dot(expert_rows, gate_cols, preferred_element_type=jnp.float32)
        up_act = jnp.dot(expert_rows, up_cols, preferred_element_type=jnp.float32)
        hidden = (jax.nn.silu(gate_act) * up_act).astype(jnp.bfloat16)
        projected = lax.dot_general(
            hidden, down_cols, (((1,), (1,)), ((), ())), preferred_element_type=jnp.float32
        )
        partials = partials.at[slot_rows].add(slot_weight[:, None] * projected)
    rounded = lax.optimization_barrier(partials.astype(jnp.bfloat16)).astype(jnp.float32)
    halved = lax.psum_scatter(
        rounded.astype(jnp.bfloat16), "tp", scatter_dimension=1, tiled=True
    ).astype(jnp.float32)
    for bit_level in reversed(range(group_bits)):
        paired_up = halved.reshape(2, -1, halved.shape[1])
        upper_half = ep_index >> bit_level & 1 == 1
        kept_part = jnp.where(upper_half, paired_up[1], paired_up[0])
        sent_part = jnp.where(upper_half, paired_up[0], paired_up[1])
        halved = kept_part + swapped(sent_part.astype(jnp.bfloat16), "ep", bit_level).astype(
            sent_part.dtype
        )
    return halved.astype(jnp.bfloat16)


def dot(a, b, dims=((1,), (0,))):
    return lax.dot_general(a, b, (dims, ((), ())), preferred_element_type=jnp.float32)


def owner_kernel(
    owners,
    info_ref,
    tok_ref,
    gate_ref,
    up_ref,
    down_ref,
    out_ref,
    info_all,
    rows_in,
    route,
    scat,
    row_w,
    x_own,
    x_far,
    gate_v,
    up_v,
    down_v,
    part_out,
    part_in,
    hid,
    proj_out,
    proj_in,
    proj_own,
    fin,
    fin_in,
    dense,
    w_sem,
    info_send,
    info_recv,
    tok_send,
    tok_recv,
    xa_sem,
    xb_sem,
    xf_sem,
    rs_send,
    rs_recv,
    ag_send,
    ag_recv,
    tp_send,
    tp_recv,
    far_sem,
    out_send,
    out_recv,
):
    ep = lax.axis_index("ep")
    t = lax.axis_index("tp")
    other_t = 1 - t
    group = ep // owners
    k = ep % owners
    base = group * owners
    far_ep = (1 - group) * owners + k
    width = tok_ref.shape[2]
    tok_rows = tok_ref.shape[1]
    share = part_in.shape[3]

    loads = [
        pltpu.make_async_copy(src, dst, w_sem.at[i])
        for i, (src, dst) in enumerate(
            ((gate_ref, gate_v), (up_ref, up_v), (down_ref, down_v))
        )
    ]
    for load in loads:
        load.start()

    barrier = pltpu.get_barrier_semaphore()
    for step in range(1, owners):
        peer = base + (k + step) % owners
        for side in range(2):
            pl.semaphore_signal(
                barrier, inc=1, device_id={"ep": peer, "tp": side}, device_id_type=MESH
            )
    pl.semaphore_signal(barrier, inc=1, device_id={"tp": other_t}, device_id_type=MESH)
    pl.semaphore_signal(barrier, inc=1, device_id={"ep": far_ep}, device_id_type=MESH)
    pl.semaphore_wait(barrier, 2 * owners)

    def remote(src, dst, send, recv, where):
        return pltpu.make_async_remote_copy(
            src_ref=src,
            dst_ref=dst,
            send_sem=send,
            recv_sem=recv,
            device_id=where,
            device_id_type=MESH,
        )

    info_copies = [
        remote(
            info_ref,
            info_all.at[k],
            info_send.at[step - 1],
            info_recv.at[step - 1],
            {"ep": base + (k + step) % owners},
        )
        for step in range(1, owners)
    ]
    for copy in info_copies:
        copy.start()

    tok_copies = []
    for block in range(4):
        to_k = 2 * t + block // 2
        to_t = block % 2
        mine = jnp.logical_and(k == to_k, t == to_t)
        tok_copies.append(
            (
                mine,
                remote(
                    tok_ref.at[block],
                    rows_in.at[k],
                    tok_send.at[block],
                    tok_recv.at[k],
                    {"ep": base + to_k, "tp": to_t},
                ),
            )
        )

        @pl.when(jnp.logical_not(mine))
        def _(copy=tok_copies[-1][1]):
            copy.start()

        @pl.when(mine)
        def _(block=block):
            pltpu.make_async_copy(tok_ref.at[block], rows_in.at[k], tok_recv.at[k]).start()

    info_all[k] = info_ref[...]
    size = owners * tok_rows
    before = jnp.where(
        lax.broadcasted_iota(jnp.int32, (size, size), 0)
        < lax.broadcasted_iota(jnp.int32, (size, size), 1),
        1.0,
        0.0,
    ).astype(jnp.bfloat16)
    for copy in info_copies:
        copy.wait_recv()
    weights = jnp.concatenate([info_all[j] for j in range(owners)], axis=1)
    chosen = jnp.where(weights > 0.0, 1.0, 0.0)
    pad = jnp.concatenate([chosen, chosen], axis=0).astype(jnp.bfloat16)
    place = dot(pad, before)[: weights.shape[0]]
    place = jnp.where(weights > 0.0, place, -1.0)
    first = group == 0
    near_place = jnp.where(first, place[0:1], place[1:2])
    far_place = jnp.where(first, place[1:2], place[0:1])
    near_w = jnp.where(first, weights[0:1], weights[1:2])
    far_w = jnp.where(first, weights[1:2], weights[0:1])
    slots = lax.broadcasted_iota(jnp.int32, (CAP, size), 0).astype(jnp.float32)
    route[0] = jnp.where(near_place == slots, 1.0, 0.0).astype(jnp.bfloat16)
    route[1] = jnp.where(far_place == slots, 1.0, 0.0).astype(jnp.bfloat16)

    for j in range(owners):
        pltpu.make_async_copy(tok_ref.at[0], rows_in.at[j], tok_recv.at[j]).wait()
    rows = rows_in[...].reshape(size, width)
    x_far_out = x_far.at[2]
    x_far_out[...] = dot(route[1], rows).astype(jnp.bfloat16)
    far_x = remote(x_far_out, x_far.at[t], xb_sem.at[0], xb_sem.at[1], {"ep": far_ep})
    far_x.start()
    x_own[t] = dot(route[0], rows).astype(jnp.bfloat16)
    own_x = remote(x_own.at[t], x_own.at[t], xa_sem.at[0], xa_sem.at[1], {"tp": other_t})
    own_x.start()

    def both(first_rows):
        return pl.ds(pl.multiple_of(first_rows * width, 16), width)

    for load in loads[:2]:
        load.wait()

    def spread(half, x_ref, wait_partner):
        near, away = both(t), both(other_t)
        gate = dot(x_ref[t], gate_v[near])
        up = dot(x_ref[t], up_v[near])
        wait_partner()
        gate = (gate + dot(x_ref[other_t], gate_v[away])).astype(jnp.bfloat16)
        up = (up + dot(x_ref[other_t], up_v[away])).astype(jnp.bfloat16)
        for j in range(owners):
            part_out[half, j, 0] = gate[j * share : (j + 1) * share]
            part_out[half, j, 1] = up[j * share : (j + 1) * share]
        copies = []
        for step in range(1, owners):
            to = (k + step) % owners
            copies.append(
                remote(
                    part_out.at[half, to],
                    part_in.at[half, step - 1],
                    rs_send.at[half, step - 1],
                    rs_recv.at[half, step - 1],
                    {"ep": base + to},
                )
            )
            copies[-1].start()
        return copies

    def activate(half, arriving):
        gate = part_out[half, k, 0].astype(jnp.float32)
        up = part_out[half, k, 1].astype(jnp.float32)
        for step in range(1, owners):
            arriving[step - 1].wait_recv()
            gate = gate + part_in[half, step - 1, 0].astype(jnp.float32)
            up = up + part_in[half, step - 1, 1].astype(jnp.float32)
        hid[half, k] = (gate / (1.0 + jnp.exp(-gate)) * up).astype(jnp.bfloat16)
        copies = []
        for step in range(1, owners):
            copies.append(
                remote(
                    hid.at[half, k],
                    hid.at[half, k],
                    ag_send.at[half, step - 1],
                    ag_recv.at[half, step - 1],
                    {"ep": base + (k + step) % owners},
                )
            )
            copies[-1].start()
        return copies

    def project(half, arriving):
        for copy in arriving:
            copy.wait_recv()
        hidden = hid[half].reshape(CAP, hid.shape[3])
        proj_out[half] = dot(hidden, down_v[both(other_t)], ((1,), (1,))).astype(jnp.bfloat16)
        copy = remote(
            proj_out.at[half],
            proj_in.at[half],
            tp_send.at[half],
            tp_recv.at[half],
            {"tp": other_t},
        )
        copy.start()
        proj_own[half] = dot(hidden, down_v[both(t)], ((1,), (1,)))
        return copy

    def settle(half, copy):
        copy.wait_recv()
        fin[half] = (proj_own[half] + proj_in[half].astype(jnp.float32)).astype(jnp.bfloat16)

    rs_a = spread(0, x_own, own_x.wait_recv)

    columns = jnp.transpose(
        jnp.concatenate([near_place, far_place, near_w, far_w, weights[: 8 - 4]], axis=0)
    )
    row_w[...] = columns
    lanes = lax.broadcasted_iota(jnp.int32, (size, CAP), 1).astype(jnp.float32)
    scat[0] = jnp.where(columns[:, 0:1] == lanes, 1.0, 0.0).astype(jnp.bfloat16)
    scat[1] = jnp.where(columns[:, 1:2] == lanes, 1.0, 0.0).astype(jnp.bfloat16)

    far_x.wait_recv()
    pass_x = remote(x_far.at[t], x_far.at[t], xf_sem.at[0], xf_sem.at[1], {"tp": other_t})
    pass_x.start()
    rs_b = spread(1, x_far, pass_x.wait_recv)
    ag_a = activate(0, rs_a)
    ag_b = activate(1, rs_b)
    loads[2].wait()
    tp_a = project(0, ag_a)
    settle(0, tp_a)
    tp_b = project(1, ag_b)
    settle(1, tp_b)
    far_y = remote(fin.at[1], fin_in, far_sem.at[0], far_sem.at[1], {"ep": far_ep})
    far_y.start()
    near_y = [
        row_w[pl.ds(j * tok_rows, tok_rows), 2:3]
        * dot(scat[0, pl.ds(j * tok_rows, tok_rows)], fin[0])
        for j in range(owners)
    ]
    far_y.wait_recv()
    spot = 2 * (k % 2) + t
    to_t = k // 2
    out_copies = []
    for j in range(owners):
        rows_j = pl.ds(j * tok_rows, tok_rows)
        far_part = row_w[rows_j, 3:4] * dot(scat[1, rows_j], fin_in[...])
        dense[j] = (near_y[j] + far_part).astype(jnp.bfloat16)
        mine = jnp.logical_and(k == j, t == to_t)
        copy = remote(
            dense.at[j],
            out_ref.at[spot],
            out_send.at[j],
            out_recv.at[spot],
            {"ep": base + j, "tp": to_t},
        )
        out_copies.append((mine, copy))

        @pl.when(jnp.logical_not(mine))
        def _(copy=copy):
            copy.start()

        @pl.when(mine)
        def _(j=j):
            pltpu.make_async_copy(dense.at[j], out_ref.at[spot], out_recv.at[spot]).start()

    for mine, copy in tok_copies + out_copies:

        @pl.when(jnp.logical_not(mine))
        def _(copy=copy):
            copy.wait_send()

    for copy in info_copies + rs_a + rs_b + ag_a + ag_b + [far_x, own_x, pass_x, tp_a, tp_b, far_y]:
        copy.wait_send()
    for block in range(4):
        pltpu.make_async_copy(dense.at[0], out_ref.at[block], out_recv.at[block]).wait()


def stay_shards(tokens, expert_ids, gate_values, group_counts, gate_weight, up_weight, down_weight):
    ep_index = lax.axis_index("ep")
    owners = lax.axis_size("ep") // WAVE
    rows, features = tokens.shape
    held, half_ff = gate_weight.shape
    width = held // 2
    blocks = features // width
    live_count = lax.dynamic_index_in_dim(group_counts, ep_index // GROUP_EP, keepdims=False)
    live = (ep_index % GROUP_EP) * rows + jnp.arange(rows, dtype=jnp.int32) < live_count
    named = expert_ids[None] == jnp.arange(8, dtype=jnp.int32)[:, None, None]
    named = jnp.logical_and(named, live[None, :, None])
    info = jnp.sum(jnp.where(named, gate_values[None], jnp.float32(0.0)), axis=2)
    cut = tokens.reshape(rows, blocks, width).transpose(1, 0, 2)
    share = CAP // owners
    size = owners * rows
    bf16, f32 = jnp.bfloat16, jnp.float32
    dma = pltpu.SemaphoreType.DMA
    anywhere = pl.BlockSpec(memory_space=pl.ANY)
    result = pl.pallas_call(
        functools.partial(owner_kernel, owners),
        out_shape=jax.ShapeDtypeStruct((blocks, rows, width), bf16),
        in_specs=[pl.BlockSpec(memory_space=pltpu.VMEM)] + [anywhere] * 4,
        out_specs=anywhere,
        scratch_shapes=[
            pltpu.VMEM((owners, 8, rows), f32),
            pltpu.VMEM((owners, rows, width), bf16),
            pltpu.VMEM((2, CAP, size), bf16),
            pltpu.VMEM((2, size, CAP), bf16),
            pltpu.VMEM((size, 8), f32),
            pltpu.VMEM((2, CAP, width), bf16),
            pltpu.VMEM((3, CAP, width), bf16),
            pltpu.VMEM((held, half_ff), bf16),
            pltpu.VMEM((held, half_ff), bf16),
            pltpu.VMEM((held, half_ff), bf16),
            pltpu.VMEM((2, owners, 2, share, half_ff), bf16),
            pltpu.VMEM((2, owners - 1, 2, share, half_ff), bf16),
            pltpu.VMEM((2, owners, share, half_ff), bf16),
            pltpu.VMEM((2, CAP, width), bf16),
            pltpu.VMEM((2, CAP, width), bf16),
            pltpu.VMEM((2, CAP, width), f32),
            pltpu.VMEM((2, CAP, width), bf16),
            pltpu.VMEM((CAP, width), bf16),
            pltpu.VMEM((owners, rows, width), bf16),
            dma((3,)),
            dma((owners - 1,)),
            dma((owners - 1,)),
            dma((4,)),
            dma((owners,)),
            dma((2,)),
            dma((2,)),
            dma((2,)),
            dma((2, owners - 1)),
            dma((2, owners - 1)),
            dma((2, owners - 1)),
            dma((2, owners - 1)),
            dma((2,)),
            dma((2,)),
            dma((2,)),
            dma((owners,)),
            dma((4,)),
        ],
        compiler_params=pltpu.CompilerParams(collective_id=0, has_side_effects=True),
    )(info, cut, gate_weight, up_weight, down_weight)
    return result.transpose(1, 0, 2).reshape(rows, features)


def shards_for(mesh):
    whole_owners = mesh.shape["ep"] == WAVE * GROUP_EP and mesh.shape["tp"] == 2
    return stay_shards if whole_owners else shards


def solution(mesh):
    placed = (
        P(("rep", "ep"), "tp"),
        P(("rep", "ep"), None),
        P(("rep", "ep"), None),
        P("rep"),
        P(("rep", "ep"), "tp"),
        P(("rep", "ep"), "tp"),
        P(("rep", "ep"), "tp"),
    )
    return jax.shard_map(
        shards_for(mesh), mesh=mesh, in_specs=placed, out_specs=P(("rep", "ep"), "tp"), check_vma=False
    )
```

```python
import functools

import jax
import jax.numpy as jnp
from jax import lax
from jax.experimental import pallas as pl
from jax.experimental.pallas import tpu as pltpu
from jax.sharding import PartitionSpec as P

D = 3584
FF = 2560
WAVE = 2
MEMBERS = 8
GROUP_EP = 4
MESH = pl.DeviceIdType.MESH
TOK_G = 512
CAP = 128


def as_sent(array):

    def short(part):
        return part.astype(jnp.bfloat16) if part.dtype == jnp.float32 else part

    return jax.tree.map(short, array)


def swapped(array, axis, distance):
    return lax.ppermute(array, axis, [(i, i ^ 1 << distance) for i in range(lax.axis_size(axis))])


def dispatch_slots(expert_ids, gate_values, live_count, expert):
    row_index = jnp.arange(TOK_G, dtype=jnp.int32)
    live_rows = row_index < live_count
    hit_mask = expert_ids == expert
    selected = jnp.logical_and(jnp.any(hit_mask, axis=1), live_rows)
    row_weight = jnp.sum(jnp.where(hit_mask, gate_values, jnp.float32(0.0)), axis=1)
    position = jnp.cumsum(selected.astype(jnp.int32)) - 1
    slot_index = jnp.arange(CAP, dtype=jnp.int32)
    slot_match = jnp.logical_and(position[None, :] == slot_index[:, None], selected[None, :])
    slot_rows = jnp.sum(jnp.where(slot_match, row_index[None, :], 0), axis=1)
    slot_valid = jnp.any(slot_match, axis=1)
    slot_weight = jnp.where(slot_valid, row_weight[slot_rows], jnp.float32(0.0))
    return (slot_rows, slot_weight)


def shards(tokens, expert_ids, gate_values, group_counts, gate_weight, up_weight, down_weight):
    ep_index = lax.axis_index("ep")
    slice_width = FF // MEMBERS
    group_bits = GROUP_EP.bit_length() - 1
    weight_stack = jnp.stack([gate_weight, up_weight, down_weight])
    rows_held = weight_stack.shape[1]
    pieces = weight_stack.shape[2] // slice_width
    slice_blocks = weight_stack.reshape(3, rows_held, pieces, slice_width).transpose(0, 2, 1, 3)
    fan_out = lax.axis_size("ep") // pieces
    outgoing = jnp.tile(slice_blocks, (1, fan_out, 1, 1))
    arrived = lax.all_to_all(outgoing, "ep", split_axis=1, concat_axis=1, tiled=True)
    columns = arrived.reshape(3, -1, slice_width)
    features = lax.all_gather(tokens, "tp", axis=1, tiled=True)
    group_data = (features, expert_ids, gate_values)
    for bit_level in range(group_bits):
        received = jax.tree.map(
            lambda part, own: part.astype(own.dtype),
            swapped(as_sent(group_data), "ep", bit_level),
            group_data,
        )
        upper_half = ep_index >> bit_level & 1 == 1
        group_data = tuple(
            (
                jnp.where(
                    upper_half, jnp.concatenate([other, own], 0), jnp.concatenate([own, other], 0)
                )
                for own, other in zip(group_data, received)
            )
        )
    group_tokens, group_ids, group_gates = group_data
    live_count = lax.dynamic_index_in_dim(group_counts, ep_index // GROUP_EP, keepdims=False)
    partials = jnp.zeros((group_tokens.shape[0], D), jnp.float32)
    for expert in range(WAVE):
        slot_rows, slot_weight = dispatch_slots(group_ids, group_gates, live_count, expert)
        expert_rows = group_tokens[slot_rows]
        gate_cols = columns[0, expert * D : (expert + 1) * D]
        up_cols = columns[1, expert * D : (expert + 1) * D]
        down_cols = columns[2, expert * D : (expert + 1) * D]
        gate_act = jnp.dot(expert_rows, gate_cols, preferred_element_type=jnp.float32)
        up_act = jnp.dot(expert_rows, up_cols, preferred_element_type=jnp.float32)
        hidden = (jax.nn.silu(gate_act) * up_act).astype(jnp.bfloat16)
        projected = lax.dot_general(
            hidden, down_cols, (((1,), (1,)), ((), ())), preferred_element_type=jnp.float32
        )
        partials = partials.at[slot_rows].add(slot_weight[:, None] * projected)
    rounded = lax.optimization_barrier(partials.astype(jnp.bfloat16)).astype(jnp.float32)
    halved = lax.psum_scatter(
        rounded.astype(jnp.bfloat16), "tp", scatter_dimension=1, tiled=True
    ).astype(jnp.float32)
    for bit_level in reversed(range(group_bits)):
        paired_up = halved.reshape(2, -1, halved.shape[1])
        upper_half = ep_index >> bit_level & 1 == 1
        kept_part = jnp.where(upper_half, paired_up[1], paired_up[0])
        sent_part = jnp.where(upper_half, paired_up[0], paired_up[1])
        halved = kept_part + swapped(sent_part.astype(jnp.bfloat16), "ep", bit_level).astype(
            sent_part.dtype
        )
    return halved.astype(jnp.bfloat16)


def dot(a, b, dims=((1,), (0,))):
    return lax.dot_general(a, b, (dims, ((), ())), preferred_element_type=jnp.float32)


def owner_kernel(
    owners,
    count_ref,
    ids_ref,
    gates_ref,
    tok_ref,
    gate_ref,
    up_ref,
    down_ref,
    out_ref,
    info,
    info_all,
    rows_in,
    route,
    scat,
    row_w,
    x_own,
    x_far,
    gate_v,
    up_v,
    down_v,
    part_out,
    part_in,
    hid,
    proj_out,
    proj_in,
    proj_own,
    fin,
    fin_in,
    dense,
    w_sem,
    info_send,
    info_recv,
    tok_send,
    tok_recv,
    xa_sem,
    xb_sem,
    xf_sem,
    rs_send,
    rs_recv,
    ag_send,
    ag_recv,
    tp_send,
    tp_recv,
    far_sem,
    out_send,
    out_recv,
):
    ep = lax.axis_index("ep")
    t = lax.axis_index("tp")
    other_t = 1 - t
    group = ep // owners
    k = ep % owners
    base = group * owners
    far_ep = (1 - group) * owners + k
    tok_rows = tok_ref.shape[0]
    held = gate_ref.shape[0]
    window = x_own.shape[2]
    shift = held - window
    rest = shift
    share = part_in.shape[3]

    loads = [
        pltpu.make_async_copy(src, dst, w_sem.at[i])
        for i, (src, dst) in enumerate(
            ((gate_ref, gate_v), (up_ref, up_v), (down_ref, down_v))
        )
    ]
    for load in loads:
        load.start()

    ids = ids_ref[...]
    row_at = lax.broadcasted_iota(jnp.int32, ids.shape, 1) + k * tok_rows
    gates = jnp.where(row_at < count_ref[group], gates_ref[...], 0.0)
    info[...] = jnp.concatenate(
        [
            jnp.sum(jnp.where(ids == expert, gates, 0.0), axis=0, keepdims=True)
            for expert in range(WAVE)
        ]
        + [jnp.zeros((8 - WAVE, tok_rows), jnp.float32)],
        axis=0,
    )

    barrier = pltpu.get_barrier_semaphore()
    for step in range(1, owners):
        peer = base + (k + step) % owners
        for side in range(2):
            pl.semaphore_signal(
                barrier, inc=1, device_id={"ep": peer, "tp": side}, device_id_type=MESH
            )
    pl.semaphore_signal(barrier, inc=1, device_id={"tp": other_t}, device_id_type=MESH)
    pl.semaphore_signal(barrier, inc=1, device_id={"ep": far_ep}, device_id_type=MESH)
    pl.semaphore_wait(barrier, 2 * owners)

    def remote(src, dst, send, recv, where):
        return pltpu.make_async_remote_copy(
            src_ref=src,
            dst_ref=dst,
            send_sem=send,
            recv_sem=recv,
            device_id=where,
            device_id_type=MESH,
        )

    info_copies = [
        remote(
            info,
            info_all.at[k],
            info_send.at[step - 1],
            info_recv.at[step - 1],
            {"ep": base + (k + step) % owners},
        )
        for step in range(1, owners)
    ]
    for copy in info_copies:
        copy.start()

    def window_of(block):
        return tok_ref.at[:, pl.ds((block // 2) * held + (block % 2) * shift, window)]

    tok_copies = []
    for block in range(4):
        to_k = 2 * t + block // 2
        to_t = block % 2
        mine = jnp.logical_and(k == to_k, t == to_t)
        tok_copies.append(
            (
                mine,
                remote(
                    window_of(block),
                    rows_in.at[k],
                    tok_send.at[block],
                    tok_recv.at[k],
                    {"ep": base + to_k, "tp": to_t},
                ),
            )
        )

        @pl.when(jnp.logical_not(mine))
        def _(copy=tok_copies[-1][1]):
            copy.start()

        @pl.when(mine)
        def _(block=block):
            pltpu.make_async_copy(window_of(block), rows_in.at[k], tok_recv.at[k]).start()

    info_all[k] = info[...]
    size = owners * tok_rows
    before = jnp.where(
        lax.broadcasted_iota(jnp.int32, (size, size), 0)
        < lax.broadcasted_iota(jnp.int32, (size, size), 1),
        1.0,
        0.0,
    ).astype(jnp.bfloat16)
    for copy in info_copies:
        copy.wait_recv()
    weights = jnp.concatenate([info_all[j] for j in range(owners)], axis=1)
    chosen = jnp.where(weights > 0.0, 1.0, 0.0)
    pad = jnp.concatenate([chosen, chosen], axis=0).astype(jnp.bfloat16)
    place = dot(pad, before)[: weights.shape[0]]
    place = jnp.where(weights > 0.0, place, -1.0)
    first = group == 0
    near_place = jnp.where(first, place[0:1], place[1:2])
    far_place = jnp.where(first, place[1:2], place[0:1])
    near_w = jnp.where(first, weights[0:1], weights[1:2])
    far_w = jnp.where(first, weights[1:2], weights[0:1])
    slots = lax.broadcasted_iota(jnp.int32, (CAP, size), 0).astype(jnp.float32)
    route[0] = jnp.where(near_place == slots, 1.0, 0.0).astype(jnp.bfloat16)
    route[1] = jnp.where(far_place == slots, 1.0, 0.0).astype(jnp.bfloat16)

    for j in range(owners):
        pltpu.make_async_copy(window_of(0), rows_in.at[j], tok_recv.at[j]).wait()
    rows = rows_in[...].reshape(size, window)
    x_far_out = x_far.at[2]
    x_far_out[...] = dot(route[1], rows).astype(jnp.bfloat16)
    far_x = remote(x_far_out, x_far.at[t], xb_sem.at[0], xb_sem.at[1], {"ep": far_ep})
    far_x.start()
    x_own[t] = dot(route[0], rows).astype(jnp.bfloat16)
    own_x = remote(x_own.at[t], x_own.at[t], xa_sem.at[0], xa_sem.at[1], {"tp": other_t})
    own_x.start()

    def span(side):
        return pl.ds(pl.multiple_of(side * shift, 128), window)

    for load in loads[:2]:
        load.wait()

    def spread(half, x_ref, wait_partner):
        near = span(t)
        away = pl.ds(pl.multiple_of(other_t * window, 128), rest)
        lanes = pl.ds(pl.multiple_of(other_t * (window - rest), 128), rest)
        gate = dot(x_ref[t], gate_v[near])
        up = dot(x_ref[t], up_v[near])
        wait_partner()
        gate = (gate + dot(x_ref[other_t, :, lanes], gate_v[away])).astype(jnp.bfloat16)
        up = (up + dot(x_ref[other_t, :, lanes], up_v[away])).astype(jnp.bfloat16)
        for j in range(owners):
            part_out[half, j, 0] = gate[j * share : (j + 1) * share]
            part_out[half, j, 1] = up[j * share : (j + 1) * share]
        copies = []
        for step in range(1, owners):
            to = (k + step) % owners
            copies.append(
                remote(
                    part_out.at[half, to],
                    part_in.at[half, step - 1],
                    rs_send.at[half, step - 1],
                    rs_recv.at[half, step - 1],
                    {"ep": base + to},
                )
            )
            copies[-1].start()
        return copies

    def activate(half, arriving):
        gate = part_out[half, k, 0].astype(jnp.float32)
        up = part_out[half, k, 1].astype(jnp.float32)
        for step in range(1, owners):
            arriving[step - 1].wait_recv()
            gate = gate + part_in[half, step - 1, 0].astype(jnp.float32)
            up = up + part_in[half, step - 1, 1].astype(jnp.float32)
        hid[half, k] = (gate / (1.0 + jnp.exp(-gate)) * up).astype(jnp.bfloat16)
        copies = []
        for step in range(1, owners):
            copies.append(
                remote(
                    hid.at[half, k],
                    hid.at[half, k],
                    ag_send.at[half, step - 1],
                    ag_recv.at[half, step - 1],
                    {"ep": base + (k + step) % owners},
                )
            )
            copies[-1].start()
        return copies

    def project(half, arriving):
        for copy in arriving:
            copy.wait_recv()
        hidden = hid[half].reshape(CAP, hid.shape[3])
        proj_out[half] = dot(hidden, down_v[span(other_t)], ((1,), (1,))).astype(jnp.bfloat16)
        copy = remote(
            proj_out.at[half],
            proj_in.at[half],
            tp_send.at[half],
            tp_recv.at[half],
            {"tp": other_t},
        )
        copy.start()
        proj_own[half] = dot(hidden, down_v[span(t)], ((1,), (1,)))
        return copy

    def settle(half, copy):
        copy.wait_recv()
        fin[half] = (proj_own[half] + proj_in[half].astype(jnp.float32)).astype(jnp.bfloat16)

    rs_a = spread(0, x_own, own_x.wait_recv)

    columns = jnp.transpose(
        jnp.concatenate([near_place, far_place, near_w, far_w, weights[: 8 - 4]], axis=0)
    )
    row_w[...] = columns
    lanes = lax.broadcasted_iota(jnp.int32, (size, CAP), 1).astype(jnp.float32)
    scat[0] = jnp.where(columns[:, 0:1] == lanes, 1.0, 0.0).astype(jnp.bfloat16)
    scat[1] = jnp.where(columns[:, 1:2] == lanes, 1.0, 0.0).astype(jnp.bfloat16)

    far_x.wait_recv()
    pass_x = remote(x_far.at[t], x_far.at[t], xf_sem.at[0], xf_sem.at[1], {"tp": other_t})
    pass_x.start()
    rs_b = spread(1, x_far, pass_x.wait_recv)
    ag_a = activate(0, rs_a)
    ag_b = activate(1, rs_b)
    loads[2].wait()
    tp_a = project(0, ag_a)
    settle(0, tp_a)
    tp_b = project(1, ag_b)
    settle(1, tp_b)
    far_y = remote(fin.at[1], fin_in, far_sem.at[0], far_sem.at[1], {"ep": far_ep})
    far_y.start()
    near_y = [
        row_w[pl.ds(j * tok_rows, tok_rows), 2:3]
        * dot(scat[0, pl.ds(j * tok_rows, tok_rows)], fin[0])
        for j in range(owners)
    ]
    far_y.wait_recv()
    to_t = k // 2
    out_copies = []
    starts = (0, window)
    sizes = (window, rest)
    for j in range(owners):
        rows_j = pl.ds(j * tok_rows, tok_rows)
        far_part = row_w[rows_j, 3:4] * dot(scat[1, rows_j], fin_in[...])
        dense[j] = (near_y[j] + far_part).astype(jnp.bfloat16)
        for side in range(2):
            from_lanes = pl.ds(window - sizes[side], sizes[side])
            for part in range(2):
                picked = jnp.logical_and(t == side, k % 2 == part)
                mine = jnp.logical_and(k == j, t == to_t)
                to_lanes = pl.ds(part * held + starts[side], sizes[side])
                spot = 2 * part + side
                away = jnp.logical_and(picked, jnp.logical_not(mine))
                copy = remote(
                    dense.at[j, :, from_lanes],
                    out_ref.at[:, to_lanes],
                    out_send.at[j],
                    out_recv.at[spot],
                    {"ep": base + j, "tp": to_t},
                )
                out_copies.append((away, copy))

                @pl.when(away)
                def _(copy=copy):
                    copy.start()

                @pl.when(jnp.logical_and(picked, mine))
                def _(j=j, from_lanes=from_lanes, to_lanes=to_lanes, spot=spot):
                    pltpu.make_async_copy(
                        dense.at[j, :, from_lanes], out_ref.at[:, to_lanes], out_recv.at[spot]
                    ).start()

    for away, copy in [(jnp.logical_not(mine), copy) for mine, copy in tok_copies] + out_copies:

        @pl.when(away)
        def _(copy=copy):
            copy.wait_send()

    for copy in info_copies + rs_a + rs_b + ag_a + ag_b + [far_x, own_x, pass_x, tp_a, tp_b, far_y]:
        copy.wait_send()
    for part in range(2):
        for side in range(2):
            here = pl.ds(part * held + starts[side], sizes[side])
            pltpu.make_async_copy(
                dense.at[0, :, pl.ds(0, sizes[side])], out_ref.at[:, here], out_recv.at[2 * part + side]
            ).wait()


def stay_shards(tokens, expert_ids, gate_values, group_counts, gate_weight, up_weight, down_weight):
    owners = lax.axis_size("ep") // WAVE
    rows, features = tokens.shape
    held, half_ff = gate_weight.shape
    width = (held // 2 + 127) // 128 * 128
    share = CAP // owners
    size = owners * rows
    bf16, f32 = jnp.bfloat16, jnp.float32
    dma = pltpu.SemaphoreType.DMA
    anywhere = pl.BlockSpec(memory_space=pl.ANY)
    result = pl.pallas_call(
        functools.partial(owner_kernel, owners),
        out_shape=jax.ShapeDtypeStruct((rows, features), bf16),
        in_specs=[
            pl.BlockSpec(memory_space=pltpu.SMEM),
            pl.BlockSpec(memory_space=pltpu.VMEM),
            pl.BlockSpec(memory_space=pltpu.VMEM),
        ]
        + [anywhere] * 4,
        out_specs=anywhere,
        scratch_shapes=[
            pltpu.VMEM((8, rows), f32),
            pltpu.VMEM((owners, 8, rows), f32),
            pltpu.VMEM((owners, rows, width), bf16),
            pltpu.VMEM((2, CAP, size), bf16),
            pltpu.VMEM((2, size, CAP), bf16),
            pltpu.VMEM((size, 8), f32),
            pltpu.VMEM((2, CAP, width), bf16),
            pltpu.VMEM((3, CAP, width), bf16),
            pltpu.VMEM((held, half_ff), bf16),
            pltpu.VMEM((held, half_ff), bf16),
            pltpu.VMEM((held, half_ff), bf16),
            pltpu.VMEM((2, owners, 2, share, half_ff), bf16),
            pltpu.VMEM((2, owners - 1, 2, share, half_ff), bf16),
            pltpu.VMEM((2, owners, share, half_ff), bf16),
            pltpu.VMEM((2, CAP, width), bf16),
            pltpu.VMEM((2, CAP, width), bf16),
            pltpu.VMEM((2, CAP, width), f32),
            pltpu.VMEM((2, CAP, width), bf16),
            pltpu.VMEM((CAP, width), bf16),
            pltpu.VMEM((owners, rows, width), bf16),
            dma((3,)),
            dma((owners - 1,)),
            dma((owners - 1,)),
            dma((4,)),
            dma((owners,)),
            dma((2,)),
            dma((2,)),
            dma((2,)),
            dma((2, owners - 1)),
            dma((2, owners - 1)),
            dma((2, owners - 1)),
            dma((2, owners - 1)),
            dma((2,)),
            dma((2,)),
            dma((2,)),
            dma((owners,)),
            dma((4,)),
        ],
        compiler_params=pltpu.CompilerParams(collective_id=0, has_side_effects=True),
    )(group_counts, expert_ids.T, gate_values.T, tokens, gate_weight, up_weight, down_weight)
    return result


def shards_for(mesh):
    whole_owners = mesh.shape["ep"] == WAVE * GROUP_EP and mesh.shape["tp"] == 2
    return stay_shards if whole_owners else shards


def solution(mesh):
    placed = (
        P(("rep", "ep"), "tp"),
        P(("rep", "ep"), None),
        P(("rep", "ep"), None),
        P("rep"),
        P(("rep", "ep"), "tp"),
        P(("rep", "ep"), "tp"),
        P(("rep", "ep"), "tp"),
    )
    return jax.shard_map(
        shards_for(mesh), mesh=mesh, in_specs=placed, out_specs=P(("rep", "ep"), "tp"), check_vma=False
    )
```

```python
import functools

import jax
import jax.numpy as jnp
from jax import lax
from jax.experimental import pallas as pl
from jax.experimental.pallas import tpu as pltpu
from jax.sharding import PartitionSpec as P

D = 3584
FF = 2560
WAVE = 2
MEMBERS = 8
GROUP_EP = 4
MESH = pl.DeviceIdType.MESH
TOK_G = 512
CAP = 128


def as_sent(array):

    def short(part):
        return part.astype(jnp.bfloat16) if part.dtype == jnp.float32 else part

    return jax.tree.map(short, array)


def swapped(array, axis, distance):
    return lax.ppermute(array, axis, [(i, i ^ 1 << distance) for i in range(lax.axis_size(axis))])


def dispatch_slots(expert_ids, gate_values, live_count, expert):
    row_index = jnp.arange(TOK_G, dtype=jnp.int32)
    live_rows = row_index < live_count
    hit_mask = expert_ids == expert
    selected = jnp.logical_and(jnp.any(hit_mask, axis=1), live_rows)
    row_weight = jnp.sum(jnp.where(hit_mask, gate_values, jnp.float32(0.0)), axis=1)
    position = jnp.cumsum(selected.astype(jnp.int32)) - 1
    slot_index = jnp.arange(CAP, dtype=jnp.int32)
    slot_match = jnp.logical_and(position[None, :] == slot_index[:, None], selected[None, :])
    slot_rows = jnp.sum(jnp.where(slot_match, row_index[None, :], 0), axis=1)
    slot_valid = jnp.any(slot_match, axis=1)
    slot_weight = jnp.where(slot_valid, row_weight[slot_rows], jnp.float32(0.0))
    return (slot_rows, slot_weight)


def shards(tokens, expert_ids, gate_values, group_counts, gate_weight, up_weight, down_weight):
    ep_index = lax.axis_index("ep")
    slice_width = FF // MEMBERS
    group_bits = GROUP_EP.bit_length() - 1
    weight_stack = jnp.stack([gate_weight, up_weight, down_weight])
    rows_held = weight_stack.shape[1]
    pieces = weight_stack.shape[2] // slice_width
    slice_blocks = weight_stack.reshape(3, rows_held, pieces, slice_width).transpose(0, 2, 1, 3)
    fan_out = lax.axis_size("ep") // pieces
    outgoing = jnp.tile(slice_blocks, (1, fan_out, 1, 1))
    arrived = lax.all_to_all(outgoing, "ep", split_axis=1, concat_axis=1, tiled=True)
    columns = arrived.reshape(3, -1, slice_width)
    features = lax.all_gather(tokens, "tp", axis=1, tiled=True)
    group_data = (features, expert_ids, gate_values)
    for bit_level in range(group_bits):
        received = jax.tree.map(
            lambda part, own: part.astype(own.dtype),
            swapped(as_sent(group_data), "ep", bit_level),
            group_data,
        )
        upper_half = ep_index >> bit_level & 1 == 1
        group_data = tuple(
            (
                jnp.where(
                    upper_half, jnp.concatenate([other, own], 0), jnp.concatenate([own, other], 0)
                )
                for own, other in zip(group_data, received)
            )
        )
    group_tokens, group_ids, group_gates = group_data
    live_count = lax.dynamic_index_in_dim(group_counts, ep_index // GROUP_EP, keepdims=False)
    partials = jnp.zeros((group_tokens.shape[0], D), jnp.float32)
    for expert in range(WAVE):
        slot_rows, slot_weight = dispatch_slots(group_ids, group_gates, live_count, expert)
        expert_rows = group_tokens[slot_rows]
        gate_cols = columns[0, expert * D : (expert + 1) * D]
        up_cols = columns[1, expert * D : (expert + 1) * D]
        down_cols = columns[2, expert * D : (expert + 1) * D]
        gate_act = jnp.dot(expert_rows, gate_cols, preferred_element_type=jnp.float32)
        up_act = jnp.dot(expert_rows, up_cols, preferred_element_type=jnp.float32)
        hidden = (jax.nn.silu(gate_act) * up_act).astype(jnp.bfloat16)
        projected = lax.dot_general(
            hidden, down_cols, (((1,), (1,)), ((), ())), preferred_element_type=jnp.float32
        )
        partials = partials.at[slot_rows].add(slot_weight[:, None] * projected)
    rounded = lax.optimization_barrier(partials.astype(jnp.bfloat16)).astype(jnp.float32)
    halved = lax.psum_scatter(
        rounded.astype(jnp.bfloat16), "tp", scatter_dimension=1, tiled=True
    ).astype(jnp.float32)
    for bit_level in reversed(range(group_bits)):
        paired_up = halved.reshape(2, -1, halved.shape[1])
        upper_half = ep_index >> bit_level & 1 == 1
        kept_part = jnp.where(upper_half, paired_up[1], paired_up[0])
        sent_part = jnp.where(upper_half, paired_up[0], paired_up[1])
        halved = kept_part + swapped(sent_part.astype(jnp.bfloat16), "ep", bit_level).astype(
            sent_part.dtype
        )
    return halved.astype(jnp.bfloat16)


def dot(a, b, dims=((1,), (0,))):
    return lax.dot_general(a, b, (dims, ((), ())), preferred_element_type=jnp.float32)


def owner_kernel(
    owners,
    count_ref,
    ids_ref,
    gates_ref,
    tok_ref,
    gate_ref,
    up_ref,
    down_ref,
    out_ref,
    info,
    info_all,
    rows_in,
    route,
    scat,
    row_w,
    x_own,
    x_far,
    gate_v,
    up_v,
    down_v,
    part_out,
    hop_in,
    hop_sum,
    pair_in,
    hid,
    proj_out,
    proj_in,
    proj_own,
    fin,
    fin_in,
    near_y,
    dense,
    w_sem,
    info_send,
    info_recv,
    tok_send,
    tok_recv,
    xa_sem,
    xb_sem,
    xf_sem,
    rs_send,
    rs_recv,
    ag_send,
    ag_recv,
    tp_send,
    tp_recv,
    far_sem,
    out_send,
    out_recv,
):
    ep = lax.axis_index("ep")
    t = lax.axis_index("tp")
    other_t = 1 - t
    group = ep // owners
    k = ep % owners
    base = group * owners
    far_ep = (1 - group) * owners + k
    tok_rows = tok_ref.shape[0]
    held = gate_ref.shape[0]
    window = x_own.shape[2]
    shift = held - window
    rest = shift
    share = pair_in.shape[2]
    lead = window - rest
    x_peer = base + k + 1 - 2 * (k % 2)
    z_peer = base + (k + 2) % owners
    across = owners - 1 - k

    loads = [
        pltpu.make_async_copy(src, dst, w_sem.at[i])
        for i, (src, dst) in enumerate(
            ((gate_ref, gate_v), (up_ref, up_v), (down_ref, down_v))
        )
    ]
    for load in loads:
        load.start()

    ids = ids_ref[...]
    row_at = lax.broadcasted_iota(jnp.int32, ids.shape, 1) + k * tok_rows
    gates = jnp.where(row_at < count_ref[group], gates_ref[...], 0.0)
    info[...] = jnp.concatenate(
        [
            jnp.sum(jnp.where(ids == expert, gates, 0.0), axis=0, keepdims=True)
            for expert in range(WAVE)
        ]
        + [jnp.zeros((8 - WAVE, tok_rows), jnp.float32)],
        axis=0,
    )

    barrier = pltpu.get_barrier_semaphore()
    for step in range(1, owners):
        peer = base + (k + step) % owners
        for side in range(2):
            pl.semaphore_signal(
                barrier, inc=1, device_id={"ep": peer, "tp": side}, device_id_type=MESH
            )
    pl.semaphore_signal(barrier, inc=1, device_id={"tp": other_t}, device_id_type=MESH)
    pl.semaphore_signal(barrier, inc=1, device_id={"ep": far_ep}, device_id_type=MESH)
    pl.semaphore_wait(barrier, 2 * owners)

    def remote(src, dst, send, recv, where):
        return pltpu.make_async_remote_copy(
            src_ref=src,
            dst_ref=dst,
            send_sem=send,
            recv_sem=recv,
            device_id=where,
            device_id_type=MESH,
        )

    spans = (pl.ds(0, window), pl.ds(lead, rest))

    def sided(build):
        return [(t == side, build(spans[side])) for side in range(2)]

    def each(pairs, act):
        for taken, copy in pairs:

            @pl.when(taken)
            def _(copy=copy):
                getattr(copy, act)()

    def from_partner(pairs):
        for side in range(2):

            @pl.when(other_t == side)
            def _(copy=pairs[side][1]):
                copy.wait_recv()

    info_copies = [
        remote(
            info,
            info_all.at[k],
            info_send.at[step - 1],
            info_recv.at[step - 1],
            {"ep": base + (k + step) % owners},
        )
        for step in range(1, owners)
    ]
    for copy in info_copies:
        copy.start()

    def window_of(block):
        start = (block // 2) * held + (window if block % 2 else 0)
        return tok_ref.at[:, pl.ds(start, rest if block % 2 else window)]

    tok_copies = []
    for block in range(4):
        to_k = 2 * t + block // 2
        to_t = block % 2
        mine = jnp.logical_and(k == to_k, t == to_t)
        tok_copies.append(
            (
                mine,
                remote(
                    window_of(block),
                    rows_in.at[k, :, spans[block % 2]],
                    tok_send.at[block],
                    tok_recv.at[k],
                    {"ep": base + to_k, "tp": to_t},
                ),
            )
        )

        @pl.when(jnp.logical_not(mine))
        def _(copy=tok_copies[-1][1]):
            copy.start()

        @pl.when(mine)
        def _(block=block):
            pltpu.make_async_copy(
                window_of(block), rows_in.at[k, :, spans[block % 2]], tok_recv.at[k]
            ).start()

    info_all[k] = info[...]
    size = owners * tok_rows
    before = jnp.where(
        lax.broadcasted_iota(jnp.int32, (size, size), 0)
        < lax.broadcasted_iota(jnp.int32, (size, size), 1),
        1.0,
        0.0,
    ).astype(jnp.bfloat16)
    for copy in info_copies:
        copy.wait_recv()
    weights = jnp.concatenate([info_all[j] for j in range(owners)], axis=1)
    chosen = jnp.where(weights > 0.0, 1.0, 0.0)
    pad = jnp.concatenate([chosen, chosen], axis=0).astype(jnp.bfloat16)
    place = dot(pad, before)[: weights.shape[0]]
    place = jnp.where(weights > 0.0, place, -1.0)
    first = group == 0
    near_place = jnp.where(first, place[0:1], place[1:2])
    far_place = jnp.where(first, place[1:2], place[0:1])
    near_w = jnp.where(first, weights[0:1], weights[1:2])
    far_w = jnp.where(first, weights[1:2], weights[0:1])
    slots = lax.broadcasted_iota(jnp.int32, (CAP, size), 0).astype(jnp.float32)
    route[0] = jnp.where(near_place == slots, 1.0, 0.0).astype(jnp.bfloat16)
    route[1] = jnp.where(far_place == slots, 1.0, 0.0).astype(jnp.bfloat16)

    for j in range(owners):
        for side in range(2):

            @pl.when(t == side)
            def _(j=j, side=side):
                pltpu.make_async_copy(
                    window_of(side), rows_in.at[j, :, spans[side]], tok_recv.at[j]
                ).wait()

    rows = rows_in[...].reshape(size, window)
    x_far_out = x_far.at[2]
    x_far_out[...] = dot(route[1], rows).astype(jnp.bfloat16)
    far_x = sided(
        lambda lanes: remote(
            x_far.at[2, :, lanes],
            x_far.at[t, :, lanes],
            xb_sem.at[0],
            xb_sem.at[1],
            {"ep": far_ep},
        )
    )
    each(far_x, "start")
    x_own[t] = dot(route[0], rows).astype(jnp.bfloat16)
    own_x = sided(
        lambda lanes: remote(
            x_own.at[t, :, lanes],
            x_own.at[t, :, lanes],
            xa_sem.at[0],
            xa_sem.at[1],
            {"tp": other_t},
        )
    )
    each(own_x, "start")

    def span(side, start, count):
        return pl.ds(pl.multiple_of(side * shift + start, 128), count)

    for load in loads[:2]:
        load.wait()

    def spread(half, x_ref):
        head, tail = x_ref[0], x_ref[1, :, lead:]
        for c, w_ref in enumerate((gate_v, up_v)):
            part = dot(head, w_ref[:window]) + dot(tail, w_ref[window:])
            part = part.astype(jnp.bfloat16)
            for j in range(owners):
                part_out[half, j, c] = part[j * share : (j + 1) * share]
        copies = []
        for slot in range(2):
            for c, peer in enumerate((x_peer, z_peer)):
                to = across if slot == 0 else peer - base
                copies.append(
                    remote(
                        part_out.at[half, to, c],
                        hop_in.at[half, c, slot],
                        rs_send.at[half, 2 * slot + c],
                        rs_recv.at[half, 2 * slot + c],
                        {"ep": peer},
                    )
                )
                copies[-1].start()
        return copies

    def forward(half, arriving):
        copies = []
        for c, peer in enumerate((z_peer, x_peer)):
            arriving[c].wait_recv()
            mixed = part_out[half, peer - base, c].astype(jnp.float32)
            mixed = mixed + hop_in[half, c, 0].astype(jnp.float32)
            hop_sum[half, c] = mixed.astype(jnp.bfloat16)
            copies.append(
                remote(
                    hop_sum.at[half, c],
                    pair_in.at[half, c],
                    rs_send.at[half, 4 + c],
                    rs_recv.at[half, 4 + c],
                    {"ep": peer},
                )
            )
            copies[-1].start()
        return copies

    def activate(half, arriving):
        for copy in arriving:
            copy.wait_recv()

        def total(c):
            out = part_out[half, k, c].astype(jnp.float32)
            out = out + hop_in[half, c, 1].astype(jnp.float32)
            return out + pair_in[half, c].astype(jnp.float32)

        gate = total(0)
        hid[half, k] = (gate / (1.0 + jnp.exp(-gate)) * total(1)).astype(jnp.bfloat16)
        copies = []
        for c, peer in enumerate((x_peer, z_peer)):
            copies.append(
                remote(
                    hid.at[half, k],
                    hid.at[half, k],
                    ag_send.at[half, c],
                    ag_recv.at[half, c],
                    {"ep": peer},
                )
            )
            copies[-1].start()
        return copies

    def relay(half, arriving):
        copies = []
        for c, (source, peer) in enumerate(((x_peer, z_peer), (z_peer, x_peer))):
            arriving[c].wait_recv()
            piece = hid.at[half, source - base, pl.ds(c * (share // 2), share // 2)]
            copies.append(
                remote(
                    piece,
                    piece,
                    ag_send.at[half, 2 + c],
                    ag_recv.at[half, 2 + c],
                    {"ep": peer},
                )
            )
            copies[-1].start()
        return copies

    def project(half, arriving, chunks):
        for copy in arriving:
            copy.wait_recv()
        hidden = hid[half].reshape(CAP, hid.shape[3])
        copies = []
        for start, count in chunks:
            lanes = pl.ds(start, count)
            proj_out[half, :, lanes] = dot(
                hidden, down_v[span(other_t, start, count)], ((1,), (1,))
            ).astype(jnp.bfloat16)
            copies.append(
                remote(
                    proj_out.at[half, :, lanes],
                    proj_in.at[half, :, lanes],
                    tp_send.at[half + len(copies)],
                    tp_recv.at[half + len(copies)],
                    {"tp": other_t},
                )
            )
            copies[-1].start()
        for start, count in chunks:
            proj_own[half, :, pl.ds(start, count)] = dot(
                hidden, down_v[span(t, start, count)], ((1,), (1,))
            )
        return copies

    def settle(half, copy, start, count):
        copy.wait_recv()
        lanes = pl.ds(start, count)
        fin[half, :, lanes] = (
            proj_own[half, :, lanes] + proj_in[half, :, lanes].astype(jnp.float32)
        ).astype(jnp.bfloat16)

    from_partner(own_x)
    rs_a = spread(0, x_own)

    columns = jnp.transpose(
        jnp.concatenate([near_place, far_place, near_w, far_w, weights[: 8 - 4]], axis=0)
    )
    row_w[...] = columns
    lanes = lax.broadcasted_iota(jnp.int32, (size, CAP), 1).astype(jnp.float32)
    scat[0] = jnp.where(columns[:, 0:1] == lanes, 1.0, 0.0).astype(jnp.bfloat16)
    scat[1] = jnp.where(columns[:, 1:2] == lanes, 1.0, 0.0).astype(jnp.bfloat16)

    each(far_x, "wait_recv")
    pass_x = sided(
        lambda lanes: remote(
            x_far.at[t, :, lanes],
            x_far.at[t, :, lanes],
            xf_sem.at[0],
            xf_sem.at[1],
            {"tp": other_t},
        )
    )
    each(pass_x, "start")
    sum_a = forward(0, rs_a)
    from_partner(pass_x)
    rs_b = spread(1, x_far)
    ag_a = activate(0, rs_a[2:] + sum_a)
    sum_b = forward(1, rs_b)
    more_a = relay(0, ag_a)
    ag_b = activate(1, rs_b[2:] + sum_b)
    loads[2].wait()
    tp_a = project(0, more_a, [(0, window)])
    more_b = relay(1, ag_b)
    settle(0, tp_a[0], 0, window)
    chunks = [(start, window // 2) for start in (0, window // 2)]
    tp_b = project(1, more_b, chunks)
    far_y = []
    for c, (start, count) in enumerate(chunks):
        settle(1, tp_b[c], start, count)
        for side in range(2):
            begin = max(start, side * lead)
            lanes = pl.ds(begin, start + count - begin)
            copy = remote(
                fin.at[1, :, lanes],
                fin_in.at[:, lanes],
                far_sem.at[0, c],
                far_sem.at[1, c],
                {"ep": far_ep},
            )
            far_y.append((t == side, copy))
        each(far_y[-2:], "start")
    for j in range(owners):
        rows_j = pl.ds(j * tok_rows, tok_rows)
        near_y[rows_j] = row_w[rows_j, 2:3] * dot(scat[0, rows_j], fin[0])
    to_t = k // 2
    spot = 2 * (k % 2) + t
    out_copies = []
    for c, (start, count) in enumerate(chunks):
        each(far_y[2 * c : 2 * c + 2], "wait_recv")
        within = pl.ds(start, count)
        for j in range(owners):
            rows_j = pl.ds(j * tok_rows, tok_rows)
            far_part = row_w[rows_j, 3:4] * dot(scat[1, rows_j], fin_in[:, within])
            dense[j, :, within] = (near_y[rows_j, within] + far_part).astype(jnp.bfloat16)
            mine = jnp.logical_and(k == j, t == to_t)
            for side in range(2):
                begin = max(start, side * lead)
                size_c = start + count - begin
                lanes = pl.ds(begin, size_c)
                to_lanes = pl.ds(
                    pl.multiple_of((k % 2) * held + side * shift + begin, 128), size_c
                )
                away = jnp.logical_and(t == side, jnp.logical_not(mine))
                copy = remote(
                    dense.at[j, :, lanes],
                    out_ref.at[:, to_lanes],
                    out_send.at[j, c],
                    out_recv.at[spot, c],
                    {"ep": base + j, "tp": to_t},
                )
                out_copies.append((away, copy))

                @pl.when(away)
                def _(copy=copy):
                    copy.start()

                @pl.when(jnp.logical_and(t == side, mine))
                def _(j=j, c=c, lanes=lanes, to_lanes=to_lanes):
                    pltpu.make_async_copy(
                        dense.at[j, :, lanes], out_ref.at[:, to_lanes], out_recv.at[spot, c]
                    ).start()

    for away, copy in [(jnp.logical_not(mine), copy) for mine, copy in tok_copies] + out_copies:

        @pl.when(away)
        def _(copy=copy):
            copy.wait_send()

    for pairs in (far_x, own_x, pass_x, far_y):
        each(pairs, "wait_send")
    for copy in info_copies + rs_a + rs_b + sum_a + sum_b + ag_a + ag_b + more_a + more_b:
        copy.wait_send()
    for copy in tp_a + tp_b:
        copy.wait_send()
    for c, (start, count) in enumerate(chunks):
        for part in range(2):
            for side in range(2):
                begin = max(start, side * lead)
                size_c = start + count - begin
                here = pl.ds(part * held + side * shift + begin, size_c)
                pltpu.make_async_copy(
                    dense.at[0, :, pl.ds(begin, size_c)],
                    out_ref.at[:, here],
                    out_recv.at[2 * part + side, c],
                ).wait()


def stay_shards(tokens, expert_ids, gate_values, group_counts, gate_weight, up_weight, down_weight):
    owners = lax.axis_size("ep") // WAVE
    rows, features = tokens.shape
    held, half_ff = gate_weight.shape
    width = (held // 2 + 127) // 128 * 128
    share = CAP // owners
    size = owners * rows
    bf16, f32 = jnp.bfloat16, jnp.float32
    dma = pltpu.SemaphoreType.DMA
    anywhere = pl.BlockSpec(memory_space=pl.ANY)
    result = pl.pallas_call(
        functools.partial(owner_kernel, owners),
        out_shape=jax.ShapeDtypeStruct((rows, features), bf16),
        in_specs=[
            pl.BlockSpec(memory_space=pltpu.SMEM),
            pl.BlockSpec(memory_space=pltpu.VMEM),
            pl.BlockSpec(memory_space=pltpu.VMEM),
        ]
        + [anywhere] * 4,
        out_specs=anywhere,
        scratch_shapes=[
            pltpu.VMEM((8, rows), f32),
            pltpu.VMEM((owners, 8, rows), f32),
            pltpu.VMEM((owners, rows, width), bf16),
            pltpu.VMEM((2, CAP, size), bf16),
            pltpu.VMEM((2, size, CAP), bf16),
            pltpu.VMEM((size, 8), f32),
            pltpu.VMEM((2, CAP, width), bf16),
            pltpu.VMEM((3, CAP, width), bf16),
            pltpu.VMEM((held, half_ff), bf16),
            pltpu.VMEM((held, half_ff), bf16),
            pltpu.VMEM((held, half_ff), bf16),
            pltpu.VMEM((2, owners, 2, share, half_ff), bf16),
            pltpu.VMEM((2, 2, 2, share, half_ff), bf16),
            pltpu.VMEM((2, 2, share, half_ff), bf16),
            pltpu.VMEM((2, 2, share, half_ff), bf16),
            pltpu.VMEM((2, owners, share, half_ff), bf16),
            pltpu.VMEM((2, CAP, width), bf16),
            pltpu.VMEM((2, CAP, width), bf16),
            pltpu.VMEM((2, CAP, width), f32),
            pltpu.VMEM((2, CAP, width), bf16),
            pltpu.VMEM((CAP, width), bf16),
            pltpu.VMEM((size, width), f32),
            pltpu.VMEM((owners, rows, width), bf16),
            dma((3,)),
            dma((owners - 1,)),
            dma((owners - 1,)),
            dma((4,)),
            dma((owners,)),
            dma((2,)),
            dma((2,)),
            dma((2,)),
            dma((2, 6)),
            dma((2, 6)),
            dma((2, 4)),
            dma((2, 4)),
            dma((3,)),
            dma((3,)),
            dma((2, 2)),
            dma((owners, 2)),
            dma((4, 2)),
        ],
        compiler_params=pltpu.CompilerParams(collective_id=0, has_side_effects=True),
    )(group_counts, expert_ids.T, gate_values.T, tokens, gate_weight, up_weight, down_weight)
    return result


def shards_for(mesh):
    whole_owners = mesh.shape["ep"] == WAVE * GROUP_EP and mesh.shape["tp"] == 2
    return stay_shards if whole_owners else shards


def solution(mesh):
    placed = (
        P(("rep", "ep"), "tp"),
        P(("rep", "ep"), None),
        P(("rep", "ep"), None),
        P("rep"),
        P(("rep", "ep"), "tp"),
        P(("rep", "ep"), "tp"),
        P(("rep", "ep"), "tp"),
    )
    return jax.shard_map(
        shards_for(mesh), mesh=mesh, in_specs=placed, out_specs=P(("rep", "ep"), "tp"), check_vma=False
    )
```

```python
import functools

import jax
import jax.numpy as jnp
from jax import lax
from jax.experimental import pallas as pl
from jax.experimental.pallas import tpu as pltpu
from jax.sharding import PartitionSpec as P

D = 3584
FF = 2560
WAVE = 2
MEMBERS = 8
GROUP_EP = 4
MESH = pl.DeviceIdType.MESH
TOK_G = 512
CAP = 128


def as_sent(array):

    def short(part):
        return part.astype(jnp.bfloat16) if part.dtype == jnp.float32 else part

    return jax.tree.map(short, array)


def swapped(array, axis, distance):
    return lax.ppermute(array, axis, [(i, i ^ 1 << distance) for i in range(lax.axis_size(axis))])


def dispatch_slots(expert_ids, gate_values, live_count, expert):
    row_index = jnp.arange(TOK_G, dtype=jnp.int32)
    live_rows = row_index < live_count
    hit_mask = expert_ids == expert
    selected = jnp.logical_and(jnp.any(hit_mask, axis=1), live_rows)
    row_weight = jnp.sum(jnp.where(hit_mask, gate_values, jnp.float32(0.0)), axis=1)
    position = jnp.cumsum(selected.astype(jnp.int32)) - 1
    slot_index = jnp.arange(CAP, dtype=jnp.int32)
    slot_match = jnp.logical_and(position[None, :] == slot_index[:, None], selected[None, :])
    slot_rows = jnp.sum(jnp.where(slot_match, row_index[None, :], 0), axis=1)
    slot_valid = jnp.any(slot_match, axis=1)
    slot_weight = jnp.where(slot_valid, row_weight[slot_rows], jnp.float32(0.0))
    return (slot_rows, slot_weight)


def shards(tokens, expert_ids, gate_values, group_counts, gate_weight, up_weight, down_weight):
    ep_index = lax.axis_index("ep")
    slice_width = FF // MEMBERS
    group_bits = GROUP_EP.bit_length() - 1
    weight_stack = jnp.stack([gate_weight, up_weight, down_weight])
    rows_held = weight_stack.shape[1]
    pieces = weight_stack.shape[2] // slice_width
    slice_blocks = weight_stack.reshape(3, rows_held, pieces, slice_width).transpose(0, 2, 1, 3)
    fan_out = lax.axis_size("ep") // pieces
    outgoing = jnp.tile(slice_blocks, (1, fan_out, 1, 1))
    arrived = lax.all_to_all(outgoing, "ep", split_axis=1, concat_axis=1, tiled=True)
    columns = arrived.reshape(3, -1, slice_width)
    features = lax.all_gather(tokens, "tp", axis=1, tiled=True)
    group_data = (features, expert_ids, gate_values)
    for bit_level in range(group_bits):
        received = jax.tree.map(
            lambda part, own: part.astype(own.dtype),
            swapped(as_sent(group_data), "ep", bit_level),
            group_data,
        )
        upper_half = ep_index >> bit_level & 1 == 1
        group_data = tuple(
            (
                jnp.where(
                    upper_half, jnp.concatenate([other, own], 0), jnp.concatenate([own, other], 0)
                )
                for own, other in zip(group_data, received)
            )
        )
    group_tokens, group_ids, group_gates = group_data
    live_count = lax.dynamic_index_in_dim(group_counts, ep_index // GROUP_EP, keepdims=False)
    partials = jnp.zeros((group_tokens.shape[0], D), jnp.float32)
    for expert in range(WAVE):
        slot_rows, slot_weight = dispatch_slots(group_ids, group_gates, live_count, expert)
        expert_rows = group_tokens[slot_rows]
        gate_cols = columns[0, expert * D : (expert + 1) * D]
        up_cols = columns[1, expert * D : (expert + 1) * D]
        down_cols = columns[2, expert * D : (expert + 1) * D]
        gate_act = jnp.dot(expert_rows, gate_cols, preferred_element_type=jnp.float32)
        up_act = jnp.dot(expert_rows, up_cols, preferred_element_type=jnp.float32)
        hidden = (jax.nn.silu(gate_act) * up_act).astype(jnp.bfloat16)
        projected = lax.dot_general(
            hidden, down_cols, (((1,), (1,)), ((), ())), preferred_element_type=jnp.float32
        )
        partials = partials.at[slot_rows].add(slot_weight[:, None] * projected)
    rounded = lax.optimization_barrier(partials.astype(jnp.bfloat16)).astype(jnp.float32)
    halved = lax.psum_scatter(
        rounded.astype(jnp.bfloat16), "tp", scatter_dimension=1, tiled=True
    ).astype(jnp.float32)
    for bit_level in reversed(range(group_bits)):
        paired_up = halved.reshape(2, -1, halved.shape[1])
        upper_half = ep_index >> bit_level & 1 == 1
        kept_part = jnp.where(upper_half, paired_up[1], paired_up[0])
        sent_part = jnp.where(upper_half, paired_up[0], paired_up[1])
        halved = kept_part + swapped(sent_part.astype(jnp.bfloat16), "ep", bit_level).astype(
            sent_part.dtype
        )
    return halved.astype(jnp.bfloat16)


def dot(a, b, dims=((1,), (0,))):
    return lax.dot_general(a, b, (dims, ((), ())), preferred_element_type=jnp.float32)


def owner_kernel(
    owners,
    count_ref,
    ids_ref,
    gates_ref,
    tok_ref,
    gate_ref,
    up_ref,
    down_ref,
    out_ref,
    info,
    info_all,
    rows_in,
    route,
    scat,
    row_w,
    x_own,
    x_far,
    gate_v,
    up_v,
    down_v,
    part_out,
    hop_in,
    hop_sum,
    pair_in,
    hid,
    proj_out,
    proj_in,
    proj_own,
    fin,
    fin_in,
    near_y,
    dense,
    w_sem,
    info_send,
    info_recv,
    tok_send,
    tok_recv,
    xa_sem,
    xb_sem,
    xf_sem,
    rs_send,
    rs_recv,
    ag_send,
    ag_recv,
    tp_send,
    tp_recv,
    far_sem,
    out_send,
    out_recv,
):
    ep = lax.axis_index("ep")
    t = lax.axis_index("tp")
    other_t = 1 - t
    group = ep // owners
    k = ep % owners
    base = group * owners
    far_ep = (1 - group) * owners + k
    tok_rows = tok_ref.shape[0]
    held = gate_ref.shape[0]
    window = x_own.shape[2]
    shift = held - window
    rest = shift
    share = pair_in.shape[2]
    lead = window - rest
    x_peer = base + k + 1 - 2 * (k % 2)
    z_peer = base + (k + 2) % owners
    across = owners - 1 - k

    loads = [
        pltpu.make_async_copy(src, dst, w_sem.at[i])
        for i, (src, dst) in enumerate(
            ((gate_ref, gate_v), (up_ref, up_v), (down_ref, down_v))
        )
    ]
    for load in loads:
        load.start()

    ids = ids_ref[...]
    row_at = lax.broadcasted_iota(jnp.int32, ids.shape, 1) + k * tok_rows
    gates = jnp.where(row_at < count_ref[group], gates_ref[...], 0.0)
    info[...] = jnp.concatenate(
        [
            jnp.sum(jnp.where(ids == expert, gates, 0.0), axis=0, keepdims=True)
            for expert in range(WAVE)
        ]
        + [jnp.zeros((8 - WAVE, tok_rows), jnp.float32)],
        axis=0,
    )

    barrier = pltpu.get_barrier_semaphore()
    for step in range(1, owners):
        peer = base + (k + step) % owners
        for side in range(2):
            pl.semaphore_signal(
                barrier, inc=1, device_id={"ep": peer, "tp": side}, device_id_type=MESH
            )
    pl.semaphore_signal(barrier, inc=1, device_id={"tp": other_t}, device_id_type=MESH)
    pl.semaphore_signal(barrier, inc=1, device_id={"ep": far_ep}, device_id_type=MESH)
    pl.semaphore_wait(barrier, 2 * owners)

    def remote(src, dst, send, recv, where):
        return pltpu.make_async_remote_copy(
            src_ref=src,
            dst_ref=dst,
            send_sem=send,
            recv_sem=recv,
            device_id=where,
            device_id_type=MESH,
        )

    halves = [(0, window // 2), (window // 2, window // 2)]

    def cut_at(side, start, count):
        begin = max(start, side * lead)
        return begin, start + count - begin

    def sided(build, start, count):
        return [(t == side, build(pl.ds(*cut_at(side, start, count)))) for side in range(2)]

    def each(pairs, act):
        for taken, copy in pairs:

            @pl.when(taken)
            def _(copy=copy):
                getattr(copy, act)()

    def from_partner(pairs):
        for side in range(2):

            @pl.when(other_t == side)
            def _(copy=pairs[side][1]):
                copy.wait_recv()

    info_copies = [
        remote(
            info,
            info_all.at[k],
            info_send.at[step - 1],
            info_recv.at[step - 1],
            {"ep": base + (k + step) % owners},
        )
        for step in range(1, owners)
    ]
    for copy in info_copies:
        copy.start()

    def window_of(block, begin, count):
        start = (block // 2) * held + (block % 2) * shift + begin
        return tok_ref.at[:, pl.ds(start, count)]

    tok_copies = []
    for c, half_span in enumerate(halves):
        for block in range(4):
            to_k = 2 * t + block // 2
            to_t = block % 2
            mine = jnp.logical_and(k == to_k, t == to_t)
            begin, count = cut_at(to_t, *half_span)
            source = window_of(block, begin, count)
            target = rows_in.at[k, :, pl.ds(begin, count)]
            copy = remote(
                source,
                target,
                tok_send.at[block, c],
                tok_recv.at[k, c],
                {"ep": base + to_k, "tp": to_t},
            )
            tok_copies.append((mine, copy))

            @pl.when(jnp.logical_not(mine))
            def _(copy=copy):
                copy.start()

            @pl.when(mine)
            def _(source=source, target=target, c=c):
                pltpu.make_async_copy(source, target, tok_recv.at[k, c]).start()

    info_all[k] = info[...]
    size = owners * tok_rows
    before = jnp.where(
        lax.broadcasted_iota(jnp.int32, (size, size), 0)
        < lax.broadcasted_iota(jnp.int32, (size, size), 1),
        1.0,
        0.0,
    ).astype(jnp.bfloat16)
    for copy in info_copies:
        copy.wait_recv()
    weights = jnp.concatenate([info_all[j] for j in range(owners)], axis=1)
    chosen = jnp.where(weights > 0.0, 1.0, 0.0)
    pad = jnp.concatenate([chosen, chosen], axis=0).astype(jnp.bfloat16)
    place = dot(pad, before)[: weights.shape[0]]
    place = jnp.where(weights > 0.0, place, -1.0)
    first = group == 0
    near_place = jnp.where(first, place[0:1], place[1:2])
    far_place = jnp.where(first, place[1:2], place[0:1])
    near_w = jnp.where(first, weights[0:1], weights[1:2])
    far_w = jnp.where(first, weights[1:2], weights[0:1])
    slots = lax.broadcasted_iota(jnp.int32, (CAP, size), 0).astype(jnp.float32)
    route[0] = jnp.where(near_place == slots, 1.0, 0.0).astype(jnp.bfloat16)
    route[1] = jnp.where(far_place == slots, 1.0, 0.0).astype(jnp.bfloat16)

    far_x, own_x = [], []
    for c, half_span in enumerate(halves):
        for j in range(owners):
            for side in range(2):

                @pl.when(t == side)
                def _(j=j, side=side, c=c, piece=cut_at(side, *half_span)):
                    pltpu.make_async_copy(
                        window_of(side, *piece), rows_in.at[j, :, pl.ds(*piece)], tok_recv.at[j, c]
                    ).wait()

        within = pl.ds(*half_span)
        rows = rows_in[:, :, within].reshape(size, half_span[1])
        x_far[2, :, within] = dot(route[1], rows).astype(jnp.bfloat16)
        far_x.append(
            sided(
                lambda lanes: remote(
                    x_far.at[2, :, lanes],
                    x_far.at[t, :, lanes],
                    xb_sem.at[0, c],
                    xb_sem.at[1, c],
                    {"ep": far_ep},
                ),
                *half_span,
            )
        )
        each(far_x[-1], "start")
        x_own[t, :, within] = dot(route[0], rows).astype(jnp.bfloat16)
        own_x.append(
            sided(
                lambda lanes: remote(
                    x_own.at[t, :, lanes],
                    x_own.at[t, :, lanes],
                    xa_sem.at[0, c],
                    xa_sem.at[1, c],
                    {"tp": other_t},
                ),
                *half_span,
            )
        )
        each(own_x[-1], "start")

    def span(side, start, count):
        return pl.ds(pl.multiple_of(side * shift + start, 128), count)

    for load in loads[:2]:
        load.wait()

    def spread(half, x_ref):
        head, tail = x_ref[0], x_ref[1, :, lead:]
        for c, w_ref in enumerate((gate_v, up_v)):
            part = dot(head, w_ref[:window]) + dot(tail, w_ref[window:])
            part = part.astype(jnp.bfloat16)
            for j in range(owners):
                part_out[half, j, c] = part[j * share : (j + 1) * share]
        copies = []
        for slot in range(2):
            for c, peer in enumerate((x_peer, z_peer)):
                to = across if slot == 0 else peer - base
                copies.append(
                    remote(
                        part_out.at[half, to, c],
                        hop_in.at[half, c, slot],
                        rs_send.at[half, 2 * slot + c],
                        rs_recv.at[half, 2 * slot + c],
                        {"ep": peer},
                    )
                )
                copies[-1].start()
        return copies

    def forward(half, arriving):
        copies = []
        for c, peer in enumerate((z_peer, x_peer)):
            arriving[c].wait_recv()
            mixed = part_out[half, peer - base, c].astype(jnp.float32)
            mixed = mixed + hop_in[half, c, 0].astype(jnp.float32)
            hop_sum[half, c] = mixed.astype(jnp.bfloat16)
            copies.append(
                remote(
                    hop_sum.at[half, c],
                    pair_in.at[half, c],
                    rs_send.at[half, 4 + c],
                    rs_recv.at[half, 4 + c],
                    {"ep": peer},
                )
            )
            copies[-1].start()
        return copies

    def activate(half, arriving):
        for copy in arriving:
            copy.wait_recv()

        def total(c):
            out = part_out[half, k, c].astype(jnp.float32)
            out = out + hop_in[half, c, 1].astype(jnp.float32)
            return out + pair_in[half, c].astype(jnp.float32)

        gate = total(0)
        hid[half, k] = (gate / (1.0 + jnp.exp(-gate)) * total(1)).astype(jnp.bfloat16)
        copies = []
        for c, peer in enumerate((x_peer, z_peer)):
            copies.append(
                remote(
                    hid.at[half, k],
                    hid.at[half, k],
                    ag_send.at[half, c],
                    ag_recv.at[half, c],
                    {"ep": peer},
                )
            )
            copies[-1].start()
        return copies

    def relay(half, arriving):
        copies = []
        for c, (source, peer) in enumerate(((x_peer, z_peer), (z_peer, x_peer))):
            arriving[c].wait_recv()
            piece = hid.at[half, source - base, pl.ds(c * (share // 2), share // 2)]
            copies.append(
                remote(
                    piece,
                    piece,
                    ag_send.at[half, 2 + c],
                    ag_recv.at[half, 2 + c],
                    {"ep": peer},
                )
            )
            copies[-1].start()
        return copies

    def project(half, arriving, chunks):
        for copy in arriving:
            copy.wait_recv()
        hidden = hid[half].reshape(CAP, hid.shape[3])
        copies = []
        for start, count in chunks:
            lanes = pl.ds(start, count)
            proj_out[half, :, lanes] = dot(
                hidden, down_v[span(other_t, start, count)], ((1,), (1,))
            ).astype(jnp.bfloat16)
            copies.append(
                remote(
                    proj_out.at[half, :, lanes],
                    proj_in.at[half, :, lanes],
                    tp_send.at[half + len(copies)],
                    tp_recv.at[half + len(copies)],
                    {"tp": other_t},
                )
            )
            copies[-1].start()
        for start, count in chunks:
            proj_own[half, :, pl.ds(start, count)] = dot(
                hidden, down_v[span(t, start, count)], ((1,), (1,))
            )
        return copies

    def settle(half, copy, start, count):
        copy.wait_recv()
        lanes = pl.ds(start, count)
        fin[half, :, lanes] = (
            proj_own[half, :, lanes] + proj_in[half, :, lanes].astype(jnp.float32)
        ).astype(jnp.bfloat16)

    for pairs in own_x:
        from_partner(pairs)
    rs_a = spread(0, x_own)

    columns = jnp.transpose(
        jnp.concatenate([near_place, far_place, near_w, far_w, weights[: 8 - 4]], axis=0)
    )
    row_w[...] = columns
    lanes = lax.broadcasted_iota(jnp.int32, (size, CAP), 1).astype(jnp.float32)
    scat[0] = jnp.where(columns[:, 0:1] == lanes, 1.0, 0.0).astype(jnp.bfloat16)
    scat[1] = jnp.where(columns[:, 1:2] == lanes, 1.0, 0.0).astype(jnp.bfloat16)

    pass_x = []
    for c, half_span in enumerate(halves):
        each(far_x[c], "wait_recv")
        pass_x.append(
            sided(
                lambda lanes: remote(
                    x_far.at[t, :, lanes],
                    x_far.at[t, :, lanes],
                    xf_sem.at[0, c],
                    xf_sem.at[1, c],
                    {"tp": other_t},
                ),
                *half_span,
            )
        )
        each(pass_x[-1], "start")
    sum_a = forward(0, rs_a)
    for pairs in pass_x:
        from_partner(pairs)
    rs_b = spread(1, x_far)
    ag_a = activate(0, rs_a[2:] + sum_a)
    sum_b = forward(1, rs_b)
    more_a = relay(0, ag_a)
    ag_b = activate(1, rs_b[2:] + sum_b)
    loads[2].wait()
    tp_a = project(0, more_a, [(0, window)])
    more_b = relay(1, ag_b)
    settle(0, tp_a[0], 0, window)
    tp_b = project(1, more_b, halves)
    small = window // 4
    chunks = [halves[0], (2 * small, small), (3 * small, small)]
    far_y = []
    for c, (start, count) in enumerate(chunks):
        if c < 2:
            settle(1, tp_b[c], *halves[c])
        far_y.append(
            sided(
                lambda lanes: remote(
                    fin.at[1, :, lanes],
                    fin_in.at[:, lanes],
                    far_sem.at[0, c],
                    far_sem.at[1, c],
                    {"ep": far_ep},
                ),
                start,
                count,
            )
        )
        each(far_y[-1], "start")
    for j in range(owners):
        rows_j = pl.ds(j * tok_rows, tok_rows)
        near_y[rows_j] = row_w[rows_j, 2:3] * dot(scat[0, rows_j], fin[0])
    to_t = k // 2
    spot = 2 * (k % 2) + t
    out_copies = []
    for c, (start, count) in enumerate(chunks):
        each(far_y[c], "wait_recv")
        within = pl.ds(start, count)
        for j in range(owners):
            rows_j = pl.ds(j * tok_rows, tok_rows)
            far_part = row_w[rows_j, 3:4] * dot(scat[1, rows_j], fin_in[:, within])
            dense[j, :, within] = (near_y[rows_j, within] + far_part).astype(jnp.bfloat16)
            mine = jnp.logical_and(k == j, t == to_t)
            for side in range(2):
                begin, size_c = cut_at(side, start, count)
                lanes = pl.ds(begin, size_c)
                to_lanes = pl.ds(
                    pl.multiple_of((k % 2) * held + side * shift + begin, 128), size_c
                )
                away = jnp.logical_and(t == side, jnp.logical_not(mine))
                copy = remote(
                    dense.at[j, :, lanes],
                    out_ref.at[:, to_lanes],
                    out_send.at[j, c],
                    out_recv.at[spot, c],
                    {"ep": base + j, "tp": to_t},
                )
                out_copies.append((away, copy))

                @pl.when(away)
                def _(copy=copy):
                    copy.start()

                @pl.when(jnp.logical_and(t == side, mine))
                def _(j=j, c=c, lanes=lanes, to_lanes=to_lanes):
                    pltpu.make_async_copy(
                        dense.at[j, :, lanes], out_ref.at[:, to_lanes], out_recv.at[spot, c]
                    ).start()

    for away, copy in [(jnp.logical_not(mine), copy) for mine, copy in tok_copies] + out_copies:

        @pl.when(away)
        def _(copy=copy):
            copy.wait_send()

    for pairs in far_x + own_x + pass_x + far_y:
        each(pairs, "wait_send")
    for copy in info_copies + rs_a + rs_b + sum_a + sum_b + ag_a + ag_b + more_a + more_b:
        copy.wait_send()
    for copy in tp_a + tp_b:
        copy.wait_send()
    for c, (start, count) in enumerate(chunks):
        for part in range(2):
            for side in range(2):
                begin, size_c = cut_at(side, start, count)
                here = pl.ds(part * held + side * shift + begin, size_c)
                pltpu.make_async_copy(
                    dense.at[0, :, pl.ds(begin, size_c)],
                    out_ref.at[:, here],
                    out_recv.at[2 * part + side, c],
                ).wait()


def stay_shards(tokens, expert_ids, gate_values, group_counts, gate_weight, up_weight, down_weight):
    owners = lax.axis_size("ep") // WAVE
    rows, features = tokens.shape
    held, half_ff = gate_weight.shape
    width = (held // 2 + 127) // 128 * 128
    share = CAP // owners
    size = owners * rows
    bf16, f32 = jnp.bfloat16, jnp.float32
    dma = pltpu.SemaphoreType.DMA
    anywhere = pl.BlockSpec(memory_space=pl.ANY)
    result = pl.pallas_call(
        functools.partial(owner_kernel, owners),
        out_shape=jax.ShapeDtypeStruct((rows, features), bf16),
        in_specs=[
            pl.BlockSpec(memory_space=pltpu.SMEM),
            pl.BlockSpec(memory_space=pltpu.VMEM),
            pl.BlockSpec(memory_space=pltpu.VMEM),
        ]
        + [anywhere] * 4,
        out_specs=anywhere,
        scratch_shapes=[
            pltpu.VMEM((8, rows), f32),
            pltpu.VMEM((owners, 8, rows), f32),
            pltpu.VMEM((owners, rows, width), bf16),
            pltpu.VMEM((2, CAP, size), bf16),
            pltpu.VMEM((2, size, CAP), bf16),
            pltpu.VMEM((size, 8), f32),
            pltpu.VMEM((2, CAP, width), bf16),
            pltpu.VMEM((3, CAP, width), bf16),
            pltpu.VMEM((held, half_ff), bf16),
            pltpu.VMEM((held, half_ff), bf16),
            pltpu.VMEM((held, half_ff), bf16),
            pltpu.VMEM((2, owners, 2, share, half_ff), bf16),
            pltpu.VMEM((2, 2, 2, share, half_ff), bf16),
            pltpu.VMEM((2, 2, share, half_ff), bf16),
            pltpu.VMEM((2, 2, share, half_ff), bf16),
            pltpu.VMEM((2, owners, share, half_ff), bf16),
            pltpu.VMEM((2, CAP, width), bf16),
            pltpu.VMEM((2, CAP, width), bf16),
            pltpu.VMEM((2, CAP, width), f32),
            pltpu.VMEM((2, CAP, width), bf16),
            pltpu.VMEM((CAP, width), bf16),
            pltpu.VMEM((size, width), f32),
            pltpu.VMEM((owners, rows, width), bf16),
            dma((3,)),
            dma((owners - 1,)),
            dma((owners - 1,)),
            dma((4, 2)),
            dma((owners, 2)),
            dma((2, 2)),
            dma((2, 2)),
            dma((2, 2)),
            dma((2, 6)),
            dma((2, 6)),
            dma((2, 4)),
            dma((2, 4)),
            dma((3,)),
            dma((3,)),
            dma((2, 3)),
            dma((owners, 3)),
            dma((4, 3)),
        ],
        compiler_params=pltpu.CompilerParams(collective_id=0, has_side_effects=True),
    )(group_counts, expert_ids.T, gate_values.T, tokens, gate_weight, up_weight, down_weight)
    return result


def shards_for(mesh):
    whole_owners = mesh.shape["ep"] == WAVE * GROUP_EP and mesh.shape["tp"] == 2
    return stay_shards if whole_owners else shards


def solution(mesh):
    placed = (
        P(("rep", "ep"), "tp"),
        P(("rep", "ep"), None),
        P(("rep", "ep"), None),
        P("rep"),
        P(("rep", "ep"), "tp"),
        P(("rep", "ep"), "tp"),
        P(("rep", "ep"), "tp"),
    )
    return jax.shard_map(
        shards_for(mesh), mesh=mesh, in_specs=placed, out_specs=P(("rep", "ep"), "tp"), check_vma=False
    )
```

```python
import functools

import jax
import jax.numpy as jnp
from jax import lax
from jax.experimental import pallas as pl
from jax.experimental.pallas import tpu as pltpu
from jax.sharding import PartitionSpec as P

D = 3584
FF = 2560
WAVE = 2
MEMBERS = 8
GROUP_EP = 4
MESH = pl.DeviceIdType.MESH
TOK_G = 512
CAP = 128


def as_sent(array):

    def short(part):
        return part.astype(jnp.bfloat16) if part.dtype == jnp.float32 else part

    return jax.tree.map(short, array)


def swapped(array, axis, distance):
    return lax.ppermute(array, axis, [(i, i ^ 1 << distance) for i in range(lax.axis_size(axis))])


def dispatch_slots(expert_ids, gate_values, live_count, expert):
    row_index = jnp.arange(TOK_G, dtype=jnp.int32)
    live_rows = row_index < live_count
    hit_mask = expert_ids == expert
    selected = jnp.logical_and(jnp.any(hit_mask, axis=1), live_rows)
    row_weight = jnp.sum(jnp.where(hit_mask, gate_values, jnp.float32(0.0)), axis=1)
    position = jnp.cumsum(selected.astype(jnp.int32)) - 1
    slot_index = jnp.arange(CAP, dtype=jnp.int32)
    slot_match = jnp.logical_and(position[None, :] == slot_index[:, None], selected[None, :])
    slot_rows = jnp.sum(jnp.where(slot_match, row_index[None, :], 0), axis=1)
    slot_valid = jnp.any(slot_match, axis=1)
    slot_weight = jnp.where(slot_valid, row_weight[slot_rows], jnp.float32(0.0))
    return (slot_rows, slot_weight)


def shards(tokens, expert_ids, gate_values, group_counts, gate_weight, up_weight, down_weight):
    ep_index = lax.axis_index("ep")
    slice_width = FF // MEMBERS
    group_bits = GROUP_EP.bit_length() - 1
    weight_stack = jnp.stack([gate_weight, up_weight, down_weight])
    rows_held = weight_stack.shape[1]
    pieces = weight_stack.shape[2] // slice_width
    slice_blocks = weight_stack.reshape(3, rows_held, pieces, slice_width).transpose(0, 2, 1, 3)
    fan_out = lax.axis_size("ep") // pieces
    outgoing = jnp.tile(slice_blocks, (1, fan_out, 1, 1))
    arrived = lax.all_to_all(outgoing, "ep", split_axis=1, concat_axis=1, tiled=True)
    columns = arrived.reshape(3, -1, slice_width)
    features = lax.all_gather(tokens, "tp", axis=1, tiled=True)
    group_data = (features, expert_ids, gate_values)
    for bit_level in range(group_bits):
        received = jax.tree.map(
            lambda part, own: part.astype(own.dtype),
            swapped(as_sent(group_data), "ep", bit_level),
            group_data,
        )
        upper_half = ep_index >> bit_level & 1 == 1
        group_data = tuple(
            (
                jnp.where(
                    upper_half, jnp.concatenate([other, own], 0), jnp.concatenate([own, other], 0)
                )
                for own, other in zip(group_data, received)
            )
        )
    group_tokens, group_ids, group_gates = group_data
    live_count = lax.dynamic_index_in_dim(group_counts, ep_index // GROUP_EP, keepdims=False)
    partials = jnp.zeros((group_tokens.shape[0], D), jnp.float32)
    for expert in range(WAVE):
        slot_rows, slot_weight = dispatch_slots(group_ids, group_gates, live_count, expert)
        expert_rows = group_tokens[slot_rows]
        gate_cols = columns[0, expert * D : (expert + 1) * D]
        up_cols = columns[1, expert * D : (expert + 1) * D]
        down_cols = columns[2, expert * D : (expert + 1) * D]
        gate_act = jnp.dot(expert_rows, gate_cols, preferred_element_type=jnp.float32)
        up_act = jnp.dot(expert_rows, up_cols, preferred_element_type=jnp.float32)
        hidden = (jax.nn.silu(gate_act) * up_act).astype(jnp.bfloat16)
        projected = lax.dot_general(
            hidden, down_cols, (((1,), (1,)), ((), ())), preferred_element_type=jnp.float32
        )
        partials = partials.at[slot_rows].add(slot_weight[:, None] * projected)
    rounded = lax.optimization_barrier(partials.astype(jnp.bfloat16)).astype(jnp.float32)
    halved = lax.psum_scatter(
        rounded.astype(jnp.bfloat16), "tp", scatter_dimension=1, tiled=True
    ).astype(jnp.float32)
    for bit_level in reversed(range(group_bits)):
        paired_up = halved.reshape(2, -1, halved.shape[1])
        upper_half = ep_index >> bit_level & 1 == 1
        kept_part = jnp.where(upper_half, paired_up[1], paired_up[0])
        sent_part = jnp.where(upper_half, paired_up[0], paired_up[1])
        halved = kept_part + swapped(sent_part.astype(jnp.bfloat16), "ep", bit_level).astype(
            sent_part.dtype
        )
    return halved.astype(jnp.bfloat16)


def dot(a, b, dims=((1,), (0,))):
    return lax.dot_general(a, b, (dims, ((), ())), preferred_element_type=jnp.float32)


def owner_kernel(
    owners,
    count_ref,
    ids_ref,
    gates_ref,
    tok_ref,
    gate_ref,
    up_ref,
    down_ref,
    out_ref,
    info,
    info_all,
    rows_in,
    route,
    scat,
    row_w,
    x_own,
    x_far,
    gate_v,
    up_v,
    down_v,
    part_out,
    hop_in,
    hop_sum,
    pair_in,
    hid,
    proj_out,
    proj_in,
    proj_own,
    fin,
    fin_in,
    near_y,
    dense,
    w_sem,
    info_send,
    info_recv,
    tok_send,
    tok_recv,
    xa_sem,
    xb_sem,
    xf_sem,
    rs_send,
    rs_recv,
    ag_send,
    ag_recv,
    tp_send,
    tp_recv,
    far_sem,
    out_send,
    out_recv,
):
    ep = lax.axis_index("ep")
    t = lax.axis_index("tp")
    other_t = 1 - t
    group = ep // owners
    k = ep % owners
    base = group * owners
    far_ep = (1 - group) * owners + k
    tok_rows = tok_ref.shape[0]
    held = gate_ref.shape[0]
    window = x_own.shape[2]
    shift = held - window
    rest = shift
    share = pair_in.shape[2]
    lead = window - rest
    x_peer = base + k + 1 - 2 * (k % 2)
    z_peer = base + (k + 2) % owners
    across = owners - 1 - k

    loads = [
        pltpu.make_async_copy(src, dst, w_sem.at[i])
        for i, (src, dst) in enumerate(
            ((gate_ref, gate_v), (up_ref, up_v), (down_ref, down_v))
        )
    ]
    for load in loads:
        load.start()

    ids = ids_ref[...]
    row_at = lax.broadcasted_iota(jnp.int32, ids.shape, 1) + k * tok_rows
    gates = jnp.where(row_at < count_ref[group], gates_ref[...], 0.0)
    info[...] = jnp.concatenate(
        [
            jnp.sum(jnp.where(ids == expert, gates, 0.0), axis=0, keepdims=True)
            for expert in range(WAVE)
        ]
        + [jnp.zeros((8 - WAVE, tok_rows), jnp.float32)],
        axis=0,
    )

    barrier = pltpu.get_barrier_semaphore()
    for step in range(1, owners):
        peer = base + (k + step) % owners
        for side in range(2):
            pl.semaphore_signal(
                barrier, inc=1, device_id={"ep": peer, "tp": side}, device_id_type=MESH
            )
    pl.semaphore_signal(barrier, inc=1, device_id={"tp": other_t}, device_id_type=MESH)
    pl.semaphore_signal(barrier, inc=1, device_id={"ep": far_ep}, device_id_type=MESH)
    pl.semaphore_wait(barrier, 2 * owners)

    def remote(src, dst, send, recv, where):
        return pltpu.make_async_remote_copy(
            src_ref=src,
            dst_ref=dst,
            send_sem=send,
            recv_sem=recv,
            device_id=where,
            device_id_type=MESH,
        )

    halves = [(0, window // 2), (window // 2, window // 2)]

    def cut_at(side, start, count):
        begin = max(start, side * lead)
        return begin, start + count - begin

    def sided(build, start, count):
        return [(t == side, build(pl.ds(*cut_at(side, start, count)))) for side in range(2)]

    def each(pairs, act):
        for taken, copy in pairs:

            @pl.when(taken)
            def _(copy=copy):
                getattr(copy, act)()

    def from_partner(pairs):
        for side in range(2):

            @pl.when(other_t == side)
            def _(copy=pairs[side][1]):
                copy.wait_recv()

    info_copies = [
        remote(
            info,
            info_all.at[k],
            info_send.at[step - 1],
            info_recv.at[step - 1],
            {"ep": base + (k + step) % owners},
        )
        for step in range(1, owners)
    ]
    for copy in info_copies:
        copy.start()

    def window_of(block, begin, count):
        start = (block // 2) * held + (block % 2) * shift + begin
        return tok_ref.at[:, pl.ds(start, count)]

    tok_copies = []
    for c, half_span in enumerate(halves):
        for block in range(4):
            to_k = 2 * t + block // 2
            to_t = block % 2
            mine = jnp.logical_and(k == to_k, t == to_t)
            begin, count = cut_at(to_t, *half_span)
            source = window_of(block, begin, count)
            target = rows_in.at[k, :, pl.ds(begin, count)]
            copy = remote(
                source,
                target,
                tok_send.at[block, c],
                tok_recv.at[k, c],
                {"ep": base + to_k, "tp": to_t},
            )
            tok_copies.append((mine, copy))

            @pl.when(jnp.logical_not(mine))
            def _(copy=copy):
                copy.start()

            @pl.when(mine)
            def _(source=source, target=target, c=c):
                pltpu.make_async_copy(source, target, tok_recv.at[k, c]).start()

    info_all[k] = info[...]
    size = owners * tok_rows
    before = jnp.where(
        lax.broadcasted_iota(jnp.int32, (size, size), 0)
        < lax.broadcasted_iota(jnp.int32, (size, size), 1),
        1.0,
        0.0,
    ).astype(jnp.bfloat16)
    for copy in info_copies:
        copy.wait_recv()
    weights = jnp.concatenate([info_all[j] for j in range(owners)], axis=1)
    chosen = jnp.where(weights > 0.0, 1.0, 0.0)
    pad = jnp.concatenate([chosen, chosen], axis=0).astype(jnp.bfloat16)
    place = dot(pad, before)[: weights.shape[0]]
    place = jnp.where(weights > 0.0, place, -1.0)
    first = group == 0
    near_place = jnp.where(first, place[0:1], place[1:2])
    far_place = jnp.where(first, place[1:2], place[0:1])
    near_w = jnp.where(first, weights[0:1], weights[1:2])
    far_w = jnp.where(first, weights[1:2], weights[0:1])
    slots = lax.broadcasted_iota(jnp.int32, (CAP, size), 0).astype(jnp.float32)
    route[0] = jnp.where(near_place == slots, 1.0, 0.0).astype(jnp.bfloat16)
    route[1] = jnp.where(far_place == slots, 1.0, 0.0).astype(jnp.bfloat16)

    far_x, own_x = [], []
    for c, half_span in enumerate(halves):
        for j in range(owners):
            for side in range(2):

                @pl.when(t == side)
                def _(j=j, side=side, c=c, piece=cut_at(side, *half_span)):
                    pltpu.make_async_copy(
                        window_of(side, *piece), rows_in.at[j, :, pl.ds(*piece)], tok_recv.at[j, c]
                    ).wait()

        within = pl.ds(*half_span)
        rows = rows_in[:, :, within].reshape(size, half_span[1])
        x_far[2, :, within] = dot(route[1], rows).astype(jnp.bfloat16)
        far_x.append(
            sided(
                lambda lanes: remote(
                    x_far.at[2, :, lanes],
                    x_far.at[t, :, lanes],
                    xb_sem.at[0, c],
                    xb_sem.at[1, c],
                    {"ep": far_ep},
                ),
                *half_span,
            )
        )
        each(far_x[-1], "start")
        x_own[t, :, within] = dot(route[0], rows).astype(jnp.bfloat16)
        own_x.append(
            sided(
                lambda lanes: remote(
                    x_own.at[t, :, lanes],
                    x_own.at[t, :, lanes],
                    xa_sem.at[0, c],
                    xa_sem.at[1, c],
                    {"tp": other_t},
                ),
                *half_span,
            )
        )
        each(own_x[-1], "start")

    def span(side, start, count):
        return pl.ds(pl.multiple_of(side * shift + start, 128), count)

    for load in loads[:2]:
        load.wait()

    def spread(half, x_ref):
        head, tail = x_ref[0], x_ref[1, :, lead:]
        for c, w_ref in enumerate((gate_v, up_v)):
            part = dot(head, w_ref[:window]) + dot(tail, w_ref[window:])
            part = part.astype(jnp.bfloat16)
            for j in range(owners):
                part_out[half, j, c] = part[j * share : (j + 1) * share]
        copies = []
        for slot in range(2):
            for c, peer in enumerate((x_peer, z_peer)):
                to = across if slot == 0 else peer - base
                copies.append(
                    remote(
                        part_out.at[half, to, c],
                        hop_in.at[half, c, slot],
                        rs_send.at[half, 2 * slot + c],
                        rs_recv.at[half, 2 * slot + c],
                        {"ep": peer},
                    )
                )
                copies[-1].start()
        return copies

    def forward(half, arriving):
        copies = []
        for c, peer in enumerate((z_peer, x_peer)):
            arriving[c].wait_recv()
            mixed = part_out[half, peer - base, c].astype(jnp.float32)
            mixed = mixed + hop_in[half, c, 0].astype(jnp.float32)
            hop_sum[half, c] = mixed.astype(jnp.bfloat16)
            copies.append(
                remote(
                    hop_sum.at[half, c],
                    pair_in.at[half, c],
                    rs_send.at[half, 4 + c],
                    rs_recv.at[half, 4 + c],
                    {"ep": peer},
                )
            )
            copies[-1].start()
        return copies

    def activate(half, arriving):
        for copy in arriving:
            copy.wait_recv()

        def total(c):
            out = part_out[half, k, c].astype(jnp.float32)
            out = out + hop_in[half, c, 1].astype(jnp.float32)
            return out + pair_in[half, c].astype(jnp.float32)

        gate = total(0)
        hid[half, k] = (gate / (1.0 + jnp.exp(-gate)) * total(1)).astype(jnp.bfloat16)
        copies = []
        for c, peer in enumerate((base + across, x_peer, z_peer)):
            copies.append(
                remote(
                    hid.at[half, k],
                    hid.at[half, k],
                    ag_send.at[half, c],
                    ag_recv.at[half, c],
                    {"ep": peer},
                )
            )
            copies[-1].start()
        return copies

    def project(half, arriving, chunks):
        for copy in arriving:
            copy.wait_recv()
        hidden = hid[half].reshape(CAP, hid.shape[3])
        copies = []
        for start, count in chunks:
            lanes = pl.ds(start, count)
            proj_out[half, :, lanes] = dot(
                hidden, down_v[span(other_t, start, count)], ((1,), (1,))
            ).astype(jnp.bfloat16)
            copies.append(
                remote(
                    proj_out.at[half, :, lanes],
                    proj_in.at[half, :, lanes],
                    tp_send.at[half + len(copies)],
                    tp_recv.at[half + len(copies)],
                    {"tp": other_t},
                )
            )
            copies[-1].start()
        for start, count in chunks:
            proj_own[half, :, pl.ds(start, count)] = dot(
                hidden, down_v[span(t, start, count)], ((1,), (1,))
            )
        return copies

    def settle(half, copy, start, count):
        copy.wait_recv()
        lanes = pl.ds(start, count)
        fin[half, :, lanes] = (
            proj_own[half, :, lanes] + proj_in[half, :, lanes].astype(jnp.float32)
        ).astype(jnp.bfloat16)

    for pairs in own_x:
        from_partner(pairs)
    rs_a = spread(0, x_own)

    columns = jnp.transpose(
        jnp.concatenate([near_place, far_place, near_w, far_w, weights[: 8 - 4]], axis=0)
    )
    row_w[...] = columns
    lanes = lax.broadcasted_iota(jnp.int32, (size, CAP), 1).astype(jnp.float32)
    scat[0] = jnp.where(columns[:, 0:1] == lanes, 1.0, 0.0).astype(jnp.bfloat16)
    scat[1] = jnp.where(columns[:, 1:2] == lanes, 1.0, 0.0).astype(jnp.bfloat16)

    pass_x = []
    for c, half_span in enumerate(halves):
        each(far_x[c], "wait_recv")
        pass_x.append(
            sided(
                lambda lanes: remote(
                    x_far.at[t, :, lanes],
                    x_far.at[t, :, lanes],
                    xf_sem.at[0, c],
                    xf_sem.at[1, c],
                    {"tp": other_t},
                ),
                *half_span,
            )
        )
        each(pass_x[-1], "start")
    sum_a = forward(0, rs_a)
    for pairs in pass_x:
        from_partner(pairs)
    rs_b = spread(1, x_far)
    ag_a = activate(0, rs_a[2:] + sum_a)
    sum_b = forward(1, rs_b)
    ag_b = activate(1, rs_b[2:] + sum_b)
    loads[2].wait()
    tp_a = project(0, ag_a, [(0, window)])
    settle(0, tp_a[0], 0, window)
    tp_b = project(1, ag_b, halves)
    small = window // 4
    chunks = [halves[0], (2 * small, small), (3 * small, small)]
    far_y = []
    for c, (start, count) in enumerate(chunks):
        if c < 2:
            settle(1, tp_b[c], *halves[c])
        far_y.append(
            sided(
                lambda lanes: remote(
                    fin.at[1, :, lanes],
                    fin_in.at[:, lanes],
                    far_sem.at[0, c],
                    far_sem.at[1, c],
                    {"ep": far_ep},
                ),
                start,
                count,
            )
        )
        each(far_y[-1], "start")
    for j in range(owners):
        rows_j = pl.ds(j * tok_rows, tok_rows)
        near_y[rows_j] = row_w[rows_j, 2:3] * dot(scat[0, rows_j], fin[0])
    to_t = k // 2
    spot = 2 * (k % 2) + t
    out_copies = []
    for c, (start, count) in enumerate(chunks):
        each(far_y[c], "wait_recv")
        within = pl.ds(start, count)
        for j in range(owners):
            rows_j = pl.ds(j * tok_rows, tok_rows)
            far_part = row_w[rows_j, 3:4] * dot(scat[1, rows_j], fin_in[:, within])
            dense[j, :, within] = (near_y[rows_j, within] + far_part).astype(jnp.bfloat16)
            mine = jnp.logical_and(k == j, t == to_t)
            for side in range(2):
                begin, size_c = cut_at(side, start, count)
                lanes = pl.ds(begin, size_c)
                to_lanes = pl.ds(
                    pl.multiple_of((k % 2) * held + side * shift + begin, 128), size_c
                )
                away = jnp.logical_and(t == side, jnp.logical_not(mine))
                copy = remote(
                    dense.at[j, :, lanes],
                    out_ref.at[:, to_lanes],
                    out_send.at[j, c],
                    out_recv.at[spot, c],
                    {"ep": base + j, "tp": to_t},
                )
                out_copies.append((away, copy))

                @pl.when(away)
                def _(copy=copy):
                    copy.start()

                @pl.when(jnp.logical_and(t == side, mine))
                def _(j=j, c=c, lanes=lanes, to_lanes=to_lanes):
                    pltpu.make_async_copy(
                        dense.at[j, :, lanes], out_ref.at[:, to_lanes], out_recv.at[spot, c]
                    ).start()

    for away, copy in [(jnp.logical_not(mine), copy) for mine, copy in tok_copies] + out_copies:

        @pl.when(away)
        def _(copy=copy):
            copy.wait_send()

    for pairs in far_x + own_x + pass_x + far_y:
        each(pairs, "wait_send")
    for copy in info_copies + rs_a + rs_b + sum_a + sum_b + ag_a + ag_b:
        copy.wait_send()
    for copy in tp_a + tp_b:
        copy.wait_send()
    for c, (start, count) in enumerate(chunks):
        for part in range(2):
            for side in range(2):
                begin, size_c = cut_at(side, start, count)
                here = pl.ds(part * held + side * shift + begin, size_c)
                pltpu.make_async_copy(
                    dense.at[0, :, pl.ds(begin, size_c)],
                    out_ref.at[:, here],
                    out_recv.at[2 * part + side, c],
                ).wait()


def stay_shards(tokens, expert_ids, gate_values, group_counts, gate_weight, up_weight, down_weight):
    owners = lax.axis_size("ep") // WAVE
    rows, features = tokens.shape
    held, half_ff = gate_weight.shape
    width = (held // 2 + 127) // 128 * 128
    share = CAP // owners
    size = owners * rows
    bf16, f32 = jnp.bfloat16, jnp.float32
    dma = pltpu.SemaphoreType.DMA
    anywhere = pl.BlockSpec(memory_space=pl.ANY)
    result = pl.pallas_call(
        functools.partial(owner_kernel, owners),
        out_shape=jax.ShapeDtypeStruct((rows, features), bf16),
        in_specs=[
            pl.BlockSpec(memory_space=pltpu.SMEM),
            pl.BlockSpec(memory_space=pltpu.VMEM),
            pl.BlockSpec(memory_space=pltpu.VMEM),
        ]
        + [anywhere] * 4,
        out_specs=anywhere,
        scratch_shapes=[
            pltpu.VMEM((8, rows), f32),
            pltpu.VMEM((owners, 8, rows), f32),
            pltpu.VMEM((owners, rows, width), bf16),
            pltpu.VMEM((2, CAP, size), bf16),
            pltpu.VMEM((2, size, CAP), bf16),
            pltpu.VMEM((size, 8), f32),
            pltpu.VMEM((2, CAP, width), bf16),
            pltpu.VMEM((3, CAP, width), bf16),
            pltpu.VMEM((held, half_ff), bf16),
            pltpu.VMEM((held, half_ff), bf16),
            pltpu.VMEM((held, half_ff), bf16),
            pltpu.VMEM((2, owners, 2, share, half_ff), bf16),
            pltpu.VMEM((2, 2, 2, share, half_ff), bf16),
            pltpu.VMEM((2, 2, share, half_ff), bf16),
            pltpu.VMEM((2, 2, share, half_ff), bf16),
            pltpu.VMEM((2, owners, share, half_ff), bf16),
            pltpu.VMEM((2, CAP, width), bf16),
            pltpu.VMEM((2, CAP, width), bf16),
            pltpu.VMEM((2, CAP, width), f32),
            pltpu.VMEM((2, CAP, width), bf16),
            pltpu.VMEM((CAP, width), bf16),
            pltpu.VMEM((size, width), f32),
            pltpu.VMEM((owners, rows, width), bf16),
            dma((3,)),
            dma((owners - 1,)),
            dma((owners - 1,)),
            dma((4, 2)),
            dma((owners, 2)),
            dma((2, 2)),
            dma((2, 2)),
            dma((2, 2)),
            dma((2, 6)),
            dma((2, 6)),
            dma((2, 4)),
            dma((2, 4)),
            dma((3,)),
            dma((3,)),
            dma((2, 3)),
            dma((owners, 3)),
            dma((4, 3)),
        ],
        compiler_params=pltpu.CompilerParams(collective_id=0, has_side_effects=True),
    )(group_counts, expert_ids.T, gate_values.T, tokens, gate_weight, up_weight, down_weight)
    return result


def shards_for(mesh):
    whole_owners = mesh.shape["ep"] == WAVE * GROUP_EP and mesh.shape["tp"] == 2
    return stay_shards if whole_owners else shards


def solution(mesh):
    placed = (
        P(("rep", "ep"), "tp"),
        P(("rep", "ep"), None),
        P(("rep", "ep"), None),
        P("rep"),
        P(("rep", "ep"), "tp"),
        P(("rep", "ep"), "tp"),
        P(("rep", "ep"), "tp"),
    )
    return jax.shard_map(
        shards_for(mesh), mesh=mesh, in_specs=placed, out_specs=P(("rep", "ep"), "tp"), check_vma=False
    )
```
